32 devices in a mesh: grp: 2 (over y), tm: 2 (over core), row: 8 (over z, x).
Axes of the slice: x: 2, y: 2, z: 4, core: 2. Of those that a mesh axis runs over, the one named last changes fastest.
Arguments:
- inputs: bfloat16 [8, 8, 43008], P(('grp', 'tm'), 'row'), parts along dimension 0, may hold values from -6 to 6
- weight: bfloat16 [5184, 192], replicated, may hold values from -0.078125 to 0.078125
- cotangent: bfloat16 [8, 8, 43008], P(('grp', 'tm'), 'row'), parts along dimension 0, may hold values from -6 to 6
Outputs:
- output: bfloat16 [8, 8, 43008], P(('grp', 'tm'), 'row'), parts along dimension 0
- input_grad: bfloat16 [8, 8, 43008], P(('grp', 'tm'), 'row'), parts along dimension 0
- filter_grad: bfloat16 [1990656], P(('grp', 'tm', 'row')), parts along dimension 0
The draws below stay inside these ranges and needn't reach their ends.
There are 2 independent parts, one for each index of `grp`. The reference program is written for one: setup_inputs(seed, part) draws one part's arguments, and reference() takes and returns one part's arrays. A program takes and returns all parts, laid end to end along the dimension named above; an argument that names none is the same for every part. Nothing has to cross between parts.
All inputs are finite; a program needn't handle non-finite values.
Results may differ from the reference program's by a relative error of at most 0.0051.
Values may be sent and summed in bfloat16 or wider, within the bound.
A program may use at most 64 MiB of HBM per device.

```python
import jax
import jax.numpy as jnp
from jax import lax

CH = 192
WIDTH = 224
FRAMES = 4
ROWS = 8


def levels(own_key, shape, split, least, largest):
    level, own = 1.0, jax.random.fold_in(own_key, 6)
    for position, shards_of in split:
        draws = jnp.exp(jax.random.uniform(jax.random.fold_in(own, position), (shards_of,), jnp.float32, least / len(split), largest / len(split)))
        level = level * jnp.repeat(draws, shape[position] // shards_of).reshape([-1 if axis == position else 1 for axis in range(len(shape))])
    return level


def scatter_about(key, dims, spread, limit, shards=(), held_as=jnp.bfloat16):
    level = levels(key, dims, shards, -0.22, 0.18) if shards else 1.0
    array = jax.random.normal(key, dims, jnp.float32) * spread * level
    return jnp.minimum(jnp.maximum(array, -limit), limit).astype(held_as)


def setup_inputs(seed: int = 0, part: int = 0) -> dict:
    key_of = jax.random.split(jax.random.key(seed), 4)
    own_keys = jax.random.split(jax.random.fold_in(key_of[3], part), 4)
    inputs = scatter_about(own_keys[0], (FRAMES, ROWS, WIDTH * CH), 1.0, 6.0, ((0, 2), (1, 8)))
    weight = scatter_about(key_of[1], (27 * CH, CH), (27 * CH) ** -0.5, 0.078125)
    cotangent = scatter_about(own_keys[2], (FRAMES, ROWS, WIDTH * CH), 1.0, 6.0, ((0, 2), (1, 8)))
    return dict(inputs=inputs, weight=weight, cotangent=cotangent)


def reference(inputs, weight, cotangent):
    frames = inputs.shape[0]
    rows = inputs.shape[1]
    x_four = inputs.reshape(frames, rows, WIDTH, CH)
    cot_four = cotangent.reshape(frames, rows, WIDTH, CH)
    act = jax.nn.silu(x_four.astype(jnp.float32)).astype(jnp.bfloat16)
    act_pad = jnp.pad(act, ((2, 0), (1, 1), (1, 1), (0, 0)))
    cot_pad = jnp.pad(cot_four, ((0, 2), (1, 1), (1, 1), (0, 0)))
    cot_flat = cot_four.reshape(-1, CH)
    output = jnp.zeros((frames * rows * WIDTH, CH), jnp.float32)
    grad_act = jnp.zeros((frames * rows * WIDTH, CH), jnp.float32)
    blocks = []
    for step_t in range(3):
        for step_h in range(3):
            for step_w in range(3):
                offset = ((step_t * 3 + step_h) * 3 + step_w) * CH
                kernel = weight[offset:offset + CH]
                piece = act_pad[step_t:step_t + frames, step_h:step_h + rows, step_w:step_w + WIDTH].reshape(-1, CH)
                output = output + jnp.dot(piece, kernel, preferred_element_type=jnp.float32)
                back_piece = cot_pad[2 - step_t:2 - step_t + frames, 2 - step_h:2 - step_h + rows, 2 - step_w:2 - step_w + WIDTH].reshape(-1, CH)
                grad_act = grad_act + lax.dot_general(back_piece, kernel, (((1,), (1,)), ((), ())), preferred_element_type=jnp.float32)
                blocks.append(lax.dot_general(piece, cot_flat, (((0,), (0,)), ((), ())), preferred_element_type=jnp.float32))
    x_float = x_four.reshape(-1, CH).astype(jnp.float32)
    sigma = jax.nn.sigmoid(x_float)
    input_grad = (grad_act * sigma * (1.0 + x_float * (1.0 - sigma))).astype(jnp.bfloat16)
    filter_grad = (jnp.concatenate(blocks, 0).reshape(-1) / (FRAMES * ROWS)).astype(jnp.bfloat16)
    shape = (frames, rows, WIDTH * CH)
    return output.astype(jnp.bfloat16).reshape(shape), input_grad.reshape(shape), filter_grad
```

```python
import functools

import jax
import jax.numpy as jnp
from jax import lax
from jax.experimental import pallas as pl
from jax.experimental.pallas import tpu as pltpu
from jax.sharding import PartitionSpec as P

CH = 192
WIDTH = 224
TAPS = 27
BLOCK = 2 * WIDTH


def fused_kernel(
    pairs, chunk, scale, x_ref, w_ref, c_ref, out_ref, ig_ref, fg_ref,
    act, cot, shifted, filt, outgoing, incoming, fwd, bwd, pad,
    send_sem, recv_sem, piece_send, piece_recv,
):
    f32, bf16 = jnp.float32, jnp.bfloat16
    grp, tm, row = lax.axis_index("grp"), lax.axis_index("tm"), lax.axis_index("row")
    rows = 2 * pairs
    pair, side = row // 2, row % 2
    own = 1 + side
    window = (side + pair) % 2

    def device(t, r):
        return (grp, t, r)

    barrier = pltpu.get_barrier_semaphore()
    me = tm * rows + row

    @pl.loop(1, 2 * rows)
    def _(step):
        other = lax.rem(me + step, 2 * rows)
        pl.semaphore_signal(
            barrier, inc=1, device_id=device(other // rows, other % rows),
            device_id_type=pl.DeviceIdType.MESH,
        )

    def act_at(slot, half):
        return act.at[slot, pl.ds(pl.multiple_of((half + 1) * BLOCK, 16), BLOCK), :]

    def cot_at(slot, half):
        return cot.at[slot, pl.ds(pl.multiple_of(half * BLOCK, 16), BLOCK), :]

    at = (act_at, cot_at)

    def move(array, src_slot, dst_slot, half, lane, target):
        return pltpu.make_async_remote_copy(
            src_ref=at[array](src_slot, half),
            dst_ref=at[array](dst_slot, half),
            send_sem=send_sem.at[lane],
            recv_sem=recv_sem.at[array, dst_slot, half],
            device_id=target,
            device_id_type=pl.DeviceIdType.MESH,
        )

    def arrived(array, slot, half):
        move(array, slot, slot, half, 0, sibling).wait_recv()

    sibling = device(1 - tm, row)
    partner = device(tm, 2 * pair + 1 - side)
    outer_pair = pair + 2 * side - 1
    has_outer = jnp.logical_and(outer_pair >= 0, outer_pair < pairs)
    outer_same = device(tm, 2 * outer_pair + side)
    outer_cross = device(tm, 2 * outer_pair + 1 - side)
    outer_slot = 3 * (1 - side)
    cot_slot = 3 * side
    has_before, has_after = pair > 0, pair < pairs - 1

    x = x_ref[...].astype(f32)
    act[own, pl.ds(pl.multiple_of((tm + 1) * BLOCK, 16), BLOCK), :] = (
        x * (1.0 / (1.0 + jnp.exp(-x)))
    ).astype(bf16)
    cot[own, pl.ds(pl.multiple_of(tm * BLOCK, 16), BLOCK), :] = c_ref[...]
    pl.semaphore_wait(barrier, 2 * rows - 1)

    straight = [
        move(0, own, own, tm, 2, partner),
        move(1, own, own, tm, 3, partner),
        move(0, own, own, tm, 0, sibling),
        move(1, own, own, tm, 1, sibling),
    ]
    outward = [
        move(0, own, outer_slot, tm, 4, outer_cross),
        move(1, own, outer_slot, tm, 5, outer_cross),
        move(0, own, outer_slot, tm, 6, outer_same),
    ]

    @pl.when(has_outer)
    def _():
        for copy in outward:
            copy.start()

    for copy in straight:
        copy.start()

    for slot in range(4):
        act[slot, 0:BLOCK, :] = jnp.zeros((BLOCK, CH), bf16)
        cot[slot, 2 * BLOCK : 3 * BLOCK, :] = jnp.zeros((BLOCK, CH), bf16)

    for slot, present in ((0, has_before), (3, has_after)):

        @pl.when(jnp.logical_not(present))
        def _():
            act[slot, BLOCK : 3 * BLOCK, :] = jnp.zeros((2 * BLOCK, CH), bf16)
            cot[slot, 0 : 2 * BLOCK, :] = jnp.zeros((2 * BLOCK, CH), bf16)

    pad[0:8, :] = jnp.zeros((8, CH), f32)
    pad[WIDTH + 8 : WIDTH + 16, :] = jnp.zeros((8, CH), f32)

    def tap_weight(step_t, step_h, step_w):
        offset = ((step_t * 3 + step_h) * 3 + step_w) * CH
        return w_ref[pl.ds(pl.multiple_of(offset, 16), CH), :]

    def convolve(step_h, first):
        @pl.loop(0, 3)
        def _(step_t):
            a = act[side + step_h, pl.ds(pl.multiple_of((2 * tm + step_t) * WIDTH, 16), BLOCK), :]
            c = cot[
                side + 2 - step_h,
                pl.ds(pl.multiple_of((2 * tm + 2 - step_t) * WIDTH, 16), BLOCK),
                :,
            ]
            for step_w in range(3):
                kernel = tap_weight(step_t, step_h, step_w)
                y = jnp.dot(a, kernel, preferred_element_type=f32)
                z = lax.dot_general(
                    c, kernel, (((1,), (1,)), ((), ())), preferred_element_type=f32
                )
                if first:

                    @pl.when(step_t == 0)
                    def _():
                        fwd[step_w] = y
                        bwd[step_w] = z

                    @pl.when(step_t > 0)
                    def _():
                        fwd[step_w] += y
                        bwd[step_w] += z
                else:
                    fwd[step_w] += y
                    bwd[step_w] += z

    other_slot = 2 - side
    arrived(0, own, 1 - tm)
    arrived(1, own, 1 - tm)
    convolve(1, True)

    onward = [move(0, other_slot, other_slot, tm, 7, sibling), move(1, other_slot, other_slot, tm, 8, sibling)]
    arrived(0, other_slot, tm)
    onward[0].start()
    arrived(1, other_slot, tm)
    onward[1].start()
    before = move(0, 0, 0, tm, 9, sibling)
    after = move(0, 3, 3, tm, 10, sibling)
    edge = move(1, cot_slot, cot_slot, tm, 11, sibling)

    @pl.when(has_before)
    def _():
        arrived(0, 0, tm)
        before.start()

    @pl.when(has_after)
    def _():
        arrived(0, 3, tm)
        after.start()

    @pl.when(has_outer_cot(pair, side, pairs))
    def _():
        arrived(1, cot_slot, tm)
        edge.start()

    arrived(0, other_slot, 1 - tm)
    arrived(1, other_slot, 1 - tm)

    for h in range(2):

        @pl.loop(0, 4)
        def _(frame):
            rows_of = pl.ds(pl.multiple_of(frame * WIDTH, 16), WIDTH)
            value = cot[1 + h, rows_of, :]
            pad[8 : WIDTH + 8, :] = value.astype(f32)
            shifted[0, h, rows_of, :] = pad[9 : WIDTH + 9, :].astype(bf16)
            shifted[1, h, rows_of, :] = value
            shifted[2, h, rows_of, :] = pad[7 : WIDTH + 7, :].astype(bf16)

    @pl.when(has_before)
    def _():
        arrived(0, 0, 1 - tm)

    @pl.when(has_after)
    def _():
        arrived(0, 3, 1 - tm)

    quarter = 2 * tm + window
    per_window = pairs * chunk
    held = filt.shape[0] // CH
    starts = [min(q * per_window // CH, TAPS - held) for q in range(4)]
    first_tap = jnp.int32(starts[0])
    for q in range(1, 4):
        first_tap = jnp.where(quarter == q, jnp.int32(starts[q]), first_tap)

    @pl.loop(0, held)
    def _(n):
        tap = first_tap + n
        step_t, step_h, step_w = tap // 9, (tap // 3) % 3, tap % 3
        span = pl.ds(pl.multiple_of(step_t * WIDTH, 16), 4 * WIDTH)
        total = None
        for h in range(2):
            term = lax.dot_general(
                act[h + step_h, span, :],
                shifted[step_w, h],
                (((0,), (0,)), ((), ())),
                preferred_element_type=f32,
            )
            total = term if total is None else total + term
        filt[pl.ds(pl.multiple_of(n * CH, 16), CH), :] = total

    for q in range(4):

        @pl.when(quarter == q)
        def _():
            base = q * per_window - starts[q] * CH
            for i in range(pairs):
                outgoing[i] = filt[base + i * chunk : base + (i + 1) * chunk, :].astype(bf16)

    pieces = []
    for i in range(pairs):
        owner = window * pairs + i
        piece = pltpu.make_async_remote_copy(
            src_ref=outgoing.at[i],
            dst_ref=incoming.at[pair],
            send_sem=piece_send.at[i],
            recv_sem=piece_recv.at[pair],
            device_id=device(tm, owner),
            device_id_type=pl.DeviceIdType.MESH,
        )
        pieces.append((owner, piece))

        @pl.when(owner != row)
        def _():
            piece.start()

        @pl.when(owner == row)
        def _():
            incoming[pair] = outgoing[i]

    @pl.when(has_outer_cot(pair, side, pairs))
    def _():
        arrived(1, cot_slot, 1 - tm)

    convolve(0, False)
    convolve(2, False)

    for frame in range(2):
        span = pl.ds(frame * WIDTH, WIDTH)
        inner = pl.ds(8, WIDTH)
        pad[inner, :] = fwd[0, span, :]
        value = fwd[1, span, :] + pad[7 : WIDTH + 7, :]
        pad[inner, :] = fwd[2, span, :]
        value = value + pad[9 : WIDTH + 9, :]
        out_ref[span, :] = value.astype(bf16)
        pad[inner, :] = bwd[0, span, :]
        value = bwd[1, span, :] + pad[9 : WIDTH + 9, :]
        pad[inner, :] = bwd[2, span, :]
        value = value + pad[7 : WIDTH + 7, :]
        x = x_ref[span, :].astype(f32)
        sigma = 1.0 / (1.0 + jnp.exp(-x))
        ig_ref[span, :] = (value * sigma * (1.0 + x * (1.0 - sigma))).astype(bf16)

    for source in range(pairs):
        from_row = 2 * source + (row // pairs + source) % 2

        @pl.when(from_row != row)
        def _():
            pltpu.make_async_remote_copy(
                src_ref=outgoing.at[0],
                dst_ref=incoming.at[source],
                send_sem=piece_send.at[0],
                recv_sem=piece_recv.at[source],
                device_id=sibling,
                device_id_type=pl.DeviceIdType.MESH,
            ).wait_recv()

    total = incoming[0].astype(f32)
    for source in range(1, pairs):
        total = total + incoming[source].astype(f32)
    fg_ref[...] = (total / scale).astype(bf16)

    for copy in straight + onward:
        copy.wait_send()

    @pl.when(has_outer)
    def _():
        for copy in outward:
            copy.wait_send()
        edge.wait_send()

    @pl.when(has_before)
    def _():
        before.wait_send()

    @pl.when(has_after)
    def _():
        after.wait_send()

    for owner, piece in pieces:

        @pl.when(owner != row)
        def _():
            piece.wait_send()


def has_outer_cot(pair, side, pairs):
    outer = pair + 2 * side - 1
    return jnp.logical_and(outer >= 0, outer < pairs)


def fused(inputs, weight, cotangent):
    frames, rows = inputs.shape[:2]
    tm_size, row_size = lax.axis_size("tm"), lax.axis_size("row")
    pairs = row_size // 2
    chunk = TAPS * CH // (2 * row_size)
    scale = frames * tm_size * rows * row_size
    quarter_rows = pairs * chunk
    held = max(
        -(-(q + 1) * quarter_rows // CH) - q * quarter_rows // CH for q in range(4)
    )
    vmem = pl.BlockSpec(memory_space=pltpu.VMEM)
    bf16, f32 = jnp.bfloat16, jnp.float32
    out, ig, fg = pl.pallas_call(
        functools.partial(fused_kernel, pairs, chunk, float(scale)),
        out_shape=(
            jax.ShapeDtypeStruct((BLOCK, CH), bf16),
            jax.ShapeDtypeStruct((BLOCK, CH), bf16),
            jax.ShapeDtypeStruct((chunk, CH), bf16),
        ),
        in_specs=[vmem] * 3,
        out_specs=(vmem, vmem, vmem),
        scratch_shapes=[
            pltpu.VMEM((4, 3 * BLOCK, CH), bf16),
            pltpu.VMEM((4, 3 * BLOCK, CH), bf16),
            pltpu.VMEM((3, 2, 2 * BLOCK, CH), bf16),
            pltpu.VMEM((held * CH, CH), f32),
            pltpu.VMEM((pairs, chunk, CH), bf16),
            pltpu.VMEM((pairs, chunk, CH), bf16),
            pltpu.VMEM((3, BLOCK, CH), f32),
            pltpu.VMEM((3, BLOCK, CH), f32),
            pltpu.VMEM((WIDTH + 16, CH), f32),
            pltpu.SemaphoreType.DMA((12,)),
            pltpu.SemaphoreType.DMA((2, 4, 2)),
            pltpu.SemaphoreType.DMA((pairs,)),
            pltpu.SemaphoreType.DMA((pairs,)),
        ],
        compiler_params=pltpu.CompilerParams(
            collective_id=0, has_side_effects=True, vmem_limit_bytes=48 * 1024 * 1024
        ),
    )(inputs.reshape(BLOCK, CH), weight, cotangent.reshape(BLOCK, CH))
    shape = (frames, rows, WIDTH * CH)
    return out.reshape(shape), ig.reshape(shape), fg.reshape(-1)


def passed_along(array, axis, by):
    length = lax.axis_size(axis)
    pairs = [(i, i + by) for i in range(length) if 0 <= i + by < length]
    return lax.ppermute(array, axis, pairs)


def with_halo(array, sides, width):
    for axis, dim in sides:
        size, length = (lax.axis_size(axis), array.shape[dim])
        up = [(i, (i + 1) % size) for i in range(size - 1)]
        down = [(j, i) for i, j in up]
        last = lax.slice_in_dim(array, length - width, length, axis=dim)
        first = lax.slice_in_dim(array, 0, width, axis=dim)
        before = lax.ppermute(last, axis, up)
        after = lax.ppermute(first, axis, down)
        array = jnp.concatenate([before, array, after], axis=dim)
    return array


def on_device(inputs, weight, cotangent):
    frames = inputs.shape[0]
    rows = inputs.shape[1]
    act = jax.nn.silu(inputs.astype(jnp.float32)).astype(jnp.bfloat16)
    earlier = passed_along(act, "tm", 1)
    extended = jnp.concatenate([earlier, act], 0)
    extended = with_halo(extended, (("row", 1),), 1)
    extended = extended.reshape(frames + 2, rows + 2, WIDTH, CH)
    act_pad = jnp.pad(extended, ((0, 0), (0, 0), (1, 1), (0, 0)))
    cot_four = cotangent.reshape(frames, rows, WIDTH, CH)
    cot_flat = cot_four.reshape(-1, CH)
    output = jnp.zeros((frames * rows * WIDTH, CH), jnp.float32)
    blocks = []
    for step_t in range(3):
        for step_h in range(3):
            for step_w in range(3):
                offset = ((step_t * 3 + step_h) * 3 + step_w) * CH
                kernel = weight[offset : offset + CH]
                piece = act_pad[
                    step_t : step_t + frames, step_h : step_h + rows, step_w : step_w + WIDTH
                ].reshape(-1, CH)
                output = output + jnp.dot(piece, kernel, preferred_element_type=jnp.float32)
                blocks.append(
                    lax.dot_general(
                        piece,
                        cot_flat,
                        (((0,), (0,)), ((), ())),
                        preferred_element_type=jnp.float32,
                    )
                )
    spread = jnp.zeros((frames + 2, rows + 2, WIDTH + 2, CH), jnp.float32)
    for step_t in range(3):
        slab_weight = weight[step_t * 9 * CH : (step_t + 1) * 9 * CH]
        terms = lax.dot_general(
            cot_flat, slab_weight, (((1,), (1,)), ((), ())), preferred_element_type=jnp.float32
        )
        terms = terms.reshape(frames, rows, WIDTH, 9, CH)
        slab = jnp.zeros((frames, rows + 2, WIDTH + 2, CH), jnp.float32)
        for step_h in range(3):
            for step_w in range(3):
                slab = slab + jnp.pad(
                    terms[:, :, :, step_h * 3 + step_w],
                    ((0, 0), (step_h, 2 - step_h), (step_w, 2 - step_w), (0, 0)),
                )
        spread = spread + jnp.pad(slab, ((step_t, 2 - step_t), (0, 0), (0, 0), (0, 0)))
    inner = spread[:, :, 1 : WIDTH + 1]
    from_next = passed_along(inner[:, 0:1], "row", -1)
    from_prev = passed_along(inner[:, rows + 1 : rows + 2], "row", 1)
    center = inner[:, 1 : rows + 1]
    center = center.at[:, rows - 1 : rows].add(from_next)
    center = center.at[:, 0:1].add(from_prev)
    returned = passed_along(center[0:2], "tm", -1)
    grad_act = center[2:].at[frames - 2 :].add(returned).reshape(-1, CH)
    x_float = inputs.reshape(-1, CH).astype(jnp.float32)
    sigma = jax.nn.sigmoid(x_float)
    input_grad = (grad_act * sigma * (1.0 + x_float * (1.0 - sigma))).astype(jnp.bfloat16)
    local_filter = jnp.concatenate(blocks, 0).reshape(-1)
    frame_blocks = lax.axis_size("tm")
    row_blocks = lax.axis_size("row")
    scale = frames * frame_blocks * rows * row_blocks
    share = lax.psum_scatter(local_filter, ("tm", "row"), scatter_dimension=0, tiled=True)
    filter_grad = (share / scale).astype(jnp.bfloat16)
    shape = (frames, rows, WIDTH * CH)
    return (output.astype(jnp.bfloat16).reshape(shape), input_grad.reshape(shape), filter_grad)


def either(mesh, inputs, weight, cotangent):
    size = mesh.shape["row"]
    quads = mesh.shape["tm"] == 2 and size % 2 == 0 and TAPS * CH % (2 * size) == 0
    if quads and inputs.shape[:2] == (2, 1):
        return fused(inputs, weight, cotangent)
    return on_device(inputs, weight, cotangent)


def solution(mesh):
    placed = (P(("grp", "tm"), "row", None), P(), P(("grp", "tm"), "row", None))
    return jax.shard_map(
        functools.partial(either, mesh),
        mesh=mesh,
        in_specs=placed,
        out_specs=(
            P(("grp", "tm"), "row", None),
            P(("grp", "tm"), "row", None),
            P(("grp", "tm", "row")),
        ),
        check_vma=False,
    )
```

```python
import functools

import jax
import jax.numpy as jnp
from jax import lax
from jax.experimental import pallas as pl
from jax.experimental.pallas import tpu as pltpu
from jax.sharding import PartitionSpec as P

CH = 192
WIDTH = 224
TAPS = 27
BLOCK = 2 * WIDTH
PACKED = 3 * WIDTH


def fused_kernel(
    pairs, chunk, scale, x_ref, w_ref, c_ref, out_ref, ig_ref, fg_ref,
    act, cot, packed, weight_in, taps, shifted, filt, outgoing, incoming, fwd, bwd, pad,
    weight_sem, send_sem, recv_sem, piece_send, piece_recv,
):
    f32, bf16 = jnp.float32, jnp.bfloat16
    grp, tm, row = lax.axis_index("grp"), lax.axis_index("tm"), lax.axis_index("row")
    rows = 2 * pairs
    pair, side = row // 2, row % 2
    own = 1 + side
    window = (side + pair) % 2

    def device(t, r):
        return (grp, t, r)

    fetch = pltpu.make_async_copy(w_ref, weight_in, weight_sem)
    fetch.start()

    barrier = pltpu.get_barrier_semaphore()
    me = tm * rows + row

    @pl.loop(1, 2 * rows)
    def _(step):
        other = lax.rem(me + step, 2 * rows)
        pl.semaphore_signal(
            barrier, inc=1, device_id=device(other // rows, other % rows),
            device_id_type=pl.DeviceIdType.MESH,
        )

    def half_of(array, slot, half):
        if array == 0:
            return act, pl.multiple_of((half + 1) * BLOCK, 16)
        return cot, pl.multiple_of(half * BLOCK, 16)

    def pack(array, slot, half, value):
        packed[array, slot, half, 0:BLOCK, :] = value[:, 0:128]
        packed[array, slot, half, BLOCK:PACKED, :] = jnp.concatenate(
            [value[0:WIDTH, 128:CH], value[WIDTH:BLOCK, 128:CH]], axis=1
        )

    def unpack(array, slot, half):
        ref, base = half_of(array, slot, half)
        ref[slot, pl.ds(base, BLOCK), 0:128] = packed[array, slot, half, 0:BLOCK, :]
        high = packed[array, slot, half, BLOCK:PACKED, :]
        ref[slot, pl.ds(base, WIDTH), 128:CH] = high[:, 0:64]
        ref[slot, pl.ds(pl.multiple_of(base + WIDTH, 16), WIDTH), 128:CH] = high[:, 64:128]

    def move(array, src_slot, dst_slot, half, lane, target):
        return pltpu.make_async_remote_copy(
            src_ref=packed.at[array, src_slot, half],
            dst_ref=packed.at[array, dst_slot, half],
            send_sem=send_sem.at[lane],
            recv_sem=recv_sem.at[array, dst_slot, half],
            device_id=target,
            device_id_type=pl.DeviceIdType.MESH,
        )

    def arrived(array, slot, half):
        move(array, slot, slot, half, 0, sibling).wait_recv()

    sibling = device(1 - tm, row)
    partner = device(tm, 2 * pair + 1 - side)
    outer_pair = pair + 2 * side - 1
    has_outer = jnp.logical_and(outer_pair >= 0, outer_pair < pairs)
    outer_same = device(tm, 2 * outer_pair + side)
    outer_cross = device(tm, 2 * outer_pair + 1 - side)
    outer_slot = 3 * (1 - side)
    cot_slot = 3 * side
    has_before, has_after = pair > 0, pair < pairs - 1

    x = x_ref[...].astype(f32)
    value = (x * (1.0 / (1.0 + jnp.exp(-x)))).astype(bf16)
    act[own, pl.ds(pl.multiple_of((tm + 1) * BLOCK, 16), BLOCK), :] = value
    pack(0, own, tm, value)
    value = c_ref[...]
    cot[own, pl.ds(pl.multiple_of(tm * BLOCK, 16), BLOCK), :] = value
    pack(1, own, tm, value)
    pl.semaphore_wait(barrier, 2 * rows - 1)

    straight = [
        move(0, own, own, tm, 2, partner),
        move(1, own, own, tm, 3, partner),
        move(0, own, own, tm, 0, sibling),
        move(1, own, own, tm, 1, sibling),
    ]
    outward = [
        move(0, own, outer_slot, tm, 4, outer_cross),
        move(0, own, outer_slot, tm, 6, outer_same),
        move(1, own, outer_slot, tm, 5, outer_cross),
    ]
    for copy in straight[:2]:
        copy.start()

    @pl.when(has_outer)
    def _():
        for copy in outward[:2]:
            copy.start()

    for copy in straight[2:]:
        copy.start()

    for slot in range(4):
        act[slot, 0:BLOCK, :] = jnp.zeros((BLOCK, CH), bf16)
        cot[slot, 2 * BLOCK : 3 * BLOCK, :] = jnp.zeros((BLOCK, CH), bf16)

    for slot, present in ((0, has_before), (3, has_after)):

        @pl.when(jnp.logical_not(present))
        def _():
            act[slot, BLOCK : 3 * BLOCK, :] = jnp.zeros((2 * BLOCK, CH), bf16)
            cot[slot, 0 : 2 * BLOCK, :] = jnp.zeros((2 * BLOCK, CH), bf16)

    pad[0:8, :] = jnp.zeros((8, CH), f32)
    pad[WIDTH + 8 : WIDTH + 16, :] = jnp.zeros((8, CH), f32)

    fetch.wait()
    for tap in range(TAPS):
        taps[tap] = weight_in[:, tap * CH : (tap + 1) * CH]

    def convolve(act_h, cot_h, first):
        @pl.loop(0, 3)
        def _(step_t):
            a = act[side + act_h, pl.ds(pl.multiple_of((2 * tm + step_t) * WIDTH, 16), BLOCK), :]
            c = cot[
                side + 2 - cot_h,
                pl.ds(pl.multiple_of((2 * tm + 2 - step_t) * WIDTH, 16), BLOCK),
                :,
            ]
            for step_w in range(3):
                y = lax.dot_general(
                    a,
                    taps[(step_t * 3 + act_h) * 3 + step_w],
                    (((1,), (1,)), ((), ())),
                    preferred_element_type=f32,
                )
                z = jnp.dot(
                    c, taps[(step_t * 3 + cot_h) * 3 + step_w], preferred_element_type=f32
                )
                if first:

                    @pl.when(step_t == 0)
                    def _():
                        fwd[step_w] = y
                        bwd[step_w] = z

                    @pl.when(step_t > 0)
                    def _():
                        fwd[step_w] += y
                        bwd[step_w] += z
                else:
                    fwd[step_w] += y
                    bwd[step_w] += z

    def shift(h):
        @pl.loop(0, 4)
        def _(frame):
            rows_of = pl.ds(pl.multiple_of(frame * WIDTH, 16), WIDTH)
            value = cot[1 + h, rows_of, :]
            pad[8 : WIDTH + 8, :] = value.astype(f32)
            shifted[0, h, rows_of, :] = pad[9 : WIDTH + 9, :].astype(bf16)
            shifted[1, h, rows_of, :] = value
            shifted[2, h, rows_of, :] = pad[7 : WIDTH + 7, :].astype(bf16)

    other_slot = 2 - side
    arrived(0, own, 1 - tm)
    unpack(0, own, 1 - tm)
    arrived(1, own, 1 - tm)
    unpack(1, own, 1 - tm)
    convolve(1, 1, True)
    shift(side)

    onward = [move(0, other_slot, other_slot, tm, 7, sibling), move(1, other_slot, other_slot, tm, 8, sibling)]
    before = move(0, 0, 0, tm, 9, sibling)
    after = move(0, 3, 3, tm, 10, sibling)
    edge = move(1, cot_slot, cot_slot, tm, 11, sibling)
    for array in range(2):
        arrived(array, other_slot, tm)
        onward[array].start()

    @pl.when(has_outer)
    def _():
        outward[2].start()

    for array in range(2):
        unpack(array, other_slot, tm)
    for array in range(2):
        arrived(array, other_slot, 1 - tm)
        unpack(array, other_slot, 1 - tm)
    shift(1 - side)

    quarter = 2 * tm + window
    per_window = pairs * chunk
    held = filt.shape[0] // CH
    starts = [min(q * per_window // CH, TAPS - held) for q in range(4)]
    first_tap = jnp.int32(starts[0])
    for q in range(1, 4):
        first_tap = jnp.where(quarter == q, jnp.int32(starts[q]), first_tap)

    def filter_term(n, h, slot):
        tap = first_tap + n
        span = pl.ds(pl.multiple_of((tap // 9) * WIDTH, 16), 4 * WIDTH)
        return lax.dot_general(
            act[slot, span, :],
            shifted[tap % 3, h],
            (((0,), (0,)), ((), ())),
            preferred_element_type=f32,
        )

    def inner_rows(n):
        step_h = ((first_tap + n) // 3) % 3
        here = pl.ds(pl.multiple_of(n * CH, 16), CH)
        h = jnp.where(step_h == 0, 1, 0)
        filt[here, :] = filter_term(n, h, h + step_h)

        @pl.when(step_h == 1)
        def _():
            filt[here, :] += filter_term(n, 1, 2)

    def outer_rows(n):
        step_h = ((first_tap + n) // 3) % 3
        here = pl.ds(pl.multiple_of(n * CH, 16), CH)

        @pl.when(step_h != 1)
        def _():
            h = jnp.where(step_h == 0, 0, 1)
            filt[here, :] += filter_term(n, h, h + step_h)

    pl.loop(0, held // 2)(inner_rows)

    @pl.when(has_before)
    def _():
        arrived(0, 0, tm)
        before.start()
        unpack(0, 0, tm)

    @pl.when(has_after)
    def _():
        arrived(0, 3, tm)
        after.start()
        unpack(0, 3, tm)

    pl.loop(held // 2, held)(inner_rows)

    @pl.when(has_before)
    def _():
        arrived(0, 0, 1 - tm)
        unpack(0, 0, 1 - tm)

    @pl.when(has_after)
    def _():
        arrived(0, 3, 1 - tm)
        unpack(0, 3, 1 - tm)

    pl.loop(0, held)(outer_rows)

    tall, cut = -(-chunk // 16) * 16, -(-chunk // 32) * 16
    for q in range(4):

        @pl.when(quarter == q)
        def _():
            for i in range(pairs):
                base = q * per_window - starts[q] * CH + i * chunk
                outgoing[i, 0:chunk, :] = filt[base : base + chunk, 0:128].astype(bf16)
                outgoing[i, tall : tall + cut, 0:64] = filt[base : base + cut, 128:CH].astype(bf16)
                outgoing[i, tall : tall + chunk - cut, 64:128] = filt[
                    base + cut : base + chunk, 128:CH
                ].astype(bf16)

    pieces = []
    for i in range(pairs):
        owner = window * pairs + i
        piece = pltpu.make_async_remote_copy(
            src_ref=outgoing.at[i],
            dst_ref=incoming.at[pair],
            send_sem=piece_send.at[i],
            recv_sem=piece_recv.at[pair],
            device_id=device(tm, owner),
            device_id_type=pl.DeviceIdType.MESH,
        )
        pieces.append((owner, piece))

        @pl.when(owner != row)
        def _():
            piece.start()

        @pl.when(owner == row)
        def _():
            incoming[pair] = outgoing[i]

    @pl.when(has_outer)
    def _():
        arrived(1, cot_slot, tm)
        edge.start()
        unpack(1, cot_slot, tm)

    convolve(2 - 2 * side, 2 * side, False)

    @pl.when(has_outer)
    def _():
        arrived(1, cot_slot, 1 - tm)
        unpack(1, cot_slot, 1 - tm)

    convolve(2 * side, 2 - 2 * side, False)

    for frame in range(2):
        span = pl.ds(frame * WIDTH, WIDTH)
        inner = pl.ds(8, WIDTH)
        pad[inner, :] = fwd[0, span, :]
        value = fwd[1, span, :] + pad[7 : WIDTH + 7, :]
        pad[inner, :] = fwd[2, span, :]
        value = value + pad[9 : WIDTH + 9, :]
        out_ref[span, :] = value.astype(bf16)
        pad[inner, :] = bwd[0, span, :]
        value = bwd[1, span, :] + pad[9 : WIDTH + 9, :]
        pad[inner, :] = bwd[2, span, :]
        value = value + pad[7 : WIDTH + 7, :]
        x = x_ref[span, :].astype(f32)
        sigma = 1.0 / (1.0 + jnp.exp(-x))
        ig_ref[span, :] = (value * sigma * (1.0 + x * (1.0 - sigma))).astype(bf16)

    for source in range(pairs):
        from_row = 2 * source + (row // pairs + source) % 2

        @pl.when(from_row != row)
        def _():
            pltpu.make_async_remote_copy(
                src_ref=outgoing.at[0],
                dst_ref=incoming.at[source],
                send_sem=piece_send.at[0],
                recv_sem=piece_recv.at[source],
                device_id=sibling,
                device_id_type=pl.DeviceIdType.MESH,
            ).wait_recv()

    total = incoming[0].astype(f32)
    for source in range(1, pairs):
        total = total + incoming[source].astype(f32)
    total = (total / scale).astype(bf16)
    fg_ref[:, 0:128] = total[0:chunk]
    fg_ref[0:cut, 128:CH] = total[tall : tall + cut, 0:64]
    fg_ref[cut:chunk, 128:CH] = total[tall : tall + chunk - cut, 64:128]

    for copy in straight + onward:
        copy.wait_send()

    @pl.when(has_outer)
    def _():
        for copy in outward:
            copy.wait_send()
        edge.wait_send()

    @pl.when(has_before)
    def _():
        before.wait_send()

    @pl.when(has_after)
    def _():
        after.wait_send()

    for owner, piece in pieces:

        @pl.when(owner != row)
        def _():
            piece.wait_send()


def fused(inputs, weight, cotangent):
    frames, rows = inputs.shape[:2]
    tm_size, row_size = lax.axis_size("tm"), lax.axis_size("row")
    pairs = row_size // 2
    chunk = TAPS * CH // (2 * row_size)
    scale = frames * tm_size * rows * row_size
    quarter_rows = pairs * chunk
    held = max(
        -(-(q + 1) * quarter_rows // CH) - q * quarter_rows // CH for q in range(4)
    )
    piece_rows = -(-chunk // 16) * 16 + -(-chunk // 32) * 16
    vmem = pl.BlockSpec(memory_space=pltpu.VMEM)
    bf16, f32 = jnp.bfloat16, jnp.float32
    out, ig, fg = pl.pallas_call(
        functools.partial(fused_kernel, pairs, chunk, float(scale)),
        out_shape=(
            jax.ShapeDtypeStruct((BLOCK, CH), bf16),
            jax.ShapeDtypeStruct((BLOCK, CH), bf16),
            jax.ShapeDtypeStruct((chunk, CH), bf16),
        ),
        in_specs=[vmem, pl.BlockSpec(memory_space=pl.ANY), vmem],
        out_specs=(vmem, vmem, vmem),
        scratch_shapes=[
            pltpu.VMEM((4, 3 * BLOCK, CH), bf16),
            pltpu.VMEM((4, 3 * BLOCK, CH), bf16),
            pltpu.VMEM((2, 4, 2, PACKED, 128), bf16),
            pltpu.VMEM((CH, TAPS * CH), bf16),
            pltpu.VMEM((TAPS, CH, CH), bf16),
            pltpu.VMEM((3, 2, 2 * BLOCK, CH), bf16),
            pltpu.VMEM((held * CH, CH), f32),
            pltpu.VMEM((pairs, piece_rows, 128), bf16),
            pltpu.VMEM((pairs, piece_rows, 128), bf16),
            pltpu.VMEM((3, BLOCK, CH), f32),
            pltpu.VMEM((3, BLOCK, CH), f32),
            pltpu.VMEM((WIDTH + 16, CH), f32),
            pltpu.SemaphoreType.DMA,
            pltpu.SemaphoreType.DMA((12,)),
            pltpu.SemaphoreType.DMA((2, 4, 2)),
            pltpu.SemaphoreType.DMA((pairs,)),
            pltpu.SemaphoreType.DMA((pairs,)),
        ],
        compiler_params=pltpu.CompilerParams(
            collective_id=0, has_side_effects=True, vmem_limit_bytes=48 * 1024 * 1024
        ),
    )(inputs.reshape(BLOCK, CH), weight.T, cotangent.reshape(BLOCK, CH))
    shape = (frames, rows, WIDTH * CH)
    return out.reshape(shape), ig.reshape(shape), fg.reshape(-1)


def passed_along(array, axis, by):
    length = lax.axis_size(axis)
    pairs = [(i, i + by) for i in range(length) if 0 <= i + by < length]
    return lax.ppermute(array, axis, pairs)


def with_halo(array, sides, width):
    for axis, dim in sides:
        size, length = (lax.axis_size(axis), array.shape[dim])
        up = [(i, (i + 1) % size) for i in range(size - 1)]
        down = [(j, i) for i, j in up]
        last = lax.slice_in_dim(array, length - width, length, axis=dim)
        first = lax.slice_in_dim(array, 0, width, axis=dim)
        before = lax.ppermute(last, axis, up)
        after = lax.ppermute(first, axis, down)
        array = jnp.concatenate([before, array, after], axis=dim)
    return array


def on_device(inputs, weight, cotangent):
    frames = inputs.shape[0]
    rows = inputs.shape[1]
    act = jax.nn.silu(inputs.astype(jnp.float32)).astype(jnp.bfloat16)
    earlier = passed_along(act, "tm", 1)
    extended = jnp.concatenate([earlier, act], 0)
    extended = with_halo(extended, (("row", 1),), 1)
    extended = extended.reshape(frames + 2, rows + 2, WIDTH, CH)
    act_pad = jnp.pad(extended, ((0, 0), (0, 0), (1, 1), (0, 0)))
    cot_four = cotangent.reshape(frames, rows, WIDTH, CH)
    cot_flat = cot_four.reshape(-1, CH)
    output = jnp.zeros((frames * rows * WIDTH, CH), jnp.float32)
    blocks = []
    for step_t in range(3):
        for step_h in range(3):
            for step_w in range(3):
                offset = ((step_t * 3 + step_h) * 3 + step_w) * CH
                kernel = weight[offset : offset + CH]
                piece = act_pad[
                    step_t : step_t + frames, step_h : step_h + rows, step_w : step_w + WIDTH
                ].reshape(-1, CH)
                output = output + jnp.dot(piece, kernel, preferred_element_type=jnp.float32)
                blocks.append(
                    lax.dot_general(
                        piece,
                        cot_flat,
                        (((0,), (0,)), ((), ())),
                        preferred_element_type=jnp.float32,
                    )
                )
    spread = jnp.zeros((frames + 2, rows + 2, WIDTH + 2, CH), jnp.float32)
    for step_t in range(3):
        slab_weight = weight[step_t * 9 * CH : (step_t + 1) * 9 * CH]
        terms = lax.dot_general(
            cot_flat, slab_weight, (((1,), (1,)), ((), ())), preferred_element_type=jnp.float32
        )
        terms = terms.reshape(frames, rows, WIDTH, 9, CH)
        slab = jnp.zeros((frames, rows + 2, WIDTH + 2, CH), jnp.float32)
        for step_h in range(3):
            for step_w in range(3):
                slab = slab + jnp.pad(
                    terms[:, :, :, step_h * 3 + step_w],
                    ((0, 0), (step_h, 2 - step_h), (step_w, 2 - step_w), (0, 0)),
                )
        spread = spread + jnp.pad(slab, ((step_t, 2 - step_t), (0, 0), (0, 0), (0, 0)))
    inner = spread[:, :, 1 : WIDTH + 1]
    from_next = passed_along(inner[:, 0:1], "row", -1)
    from_prev = passed_along(inner[:, rows + 1 : rows + 2], "row", 1)
    center = inner[:, 1 : rows + 1]
    center = center.at[:, rows - 1 : rows].add(from_next)
    center = center.at[:, 0:1].add(from_prev)
    returned = passed_along(center[0:2], "tm", -1)
    grad_act = center[2:].at[frames - 2 :].add(returned).reshape(-1, CH)
    x_float = inputs.reshape(-1, CH).astype(jnp.float32)
    sigma = jax.nn.sigmoid(x_float)
    input_grad = (grad_act * sigma * (1.0 + x_float * (1.0 - sigma))).astype(jnp.bfloat16)
    local_filter = jnp.concatenate(blocks, 0).reshape(-1)
    frame_blocks = lax.axis_size("tm")
    row_blocks = lax.axis_size("row")
    scale = frames * frame_blocks * rows * row_blocks
    share = lax.psum_scatter(local_filter, ("tm", "row"), scatter_dimension=0, tiled=True)
    filter_grad = (share / scale).astype(jnp.bfloat16)
    shape = (frames, rows, WIDTH * CH)
    return (output.astype(jnp.bfloat16).reshape(shape), input_grad.reshape(shape), filter_grad)


def either(mesh, inputs, weight, cotangent):
    size = mesh.shape["row"]
    quads = mesh.shape["tm"] == 2 and size % 2 == 0 and TAPS * CH % (4 * size) == 0
    if quads and inputs.shape[:2] == (2, 1):
        return fused(inputs, weight, cotangent)
    return on_device(inputs, weight, cotangent)


def solution(mesh):
    placed = (P(("grp", "tm"), "row", None), P(), P(("grp", "tm"), "row", None))
    return jax.shard_map(
        functools.partial(either, mesh),
        mesh=mesh,
        in_specs=placed,
        out_specs=(
            P(("grp", "tm"), "row", None),
            P(("grp", "tm"), "row", None),
            P(("grp", "tm", "row")),
        ),
        check_vma=False,
    )
```

```python
import functools

import jax
import jax.numpy as jnp
from jax import lax
from jax.experimental import pallas as pl
from jax.experimental.pallas import tpu as pltpu
from jax.sharding import PartitionSpec as P

CH = 192
WIDTH = 224
TAPS = 27
BLOCK = 2 * WIDTH
PACKED = 3 * WIDTH


def fused_kernel(
    pairs, chunk, scale, x_ref, w_ref, c_ref, out_ref, ig_ref, fg_ref,
    act, cot, packed, weight_in, taps, shifted, filt, outgoing, incoming, fwd, bwd, pad,
    weight_sem, send_sem, recv_sem, piece_send, piece_recv,
):
    f32, bf16 = jnp.float32, jnp.bfloat16
    grp, tm, row = lax.axis_index("grp"), lax.axis_index("tm"), lax.axis_index("row")
    rows = 2 * pairs
    pair, side = row // 2, row % 2
    own = 1 + side
    window = (side + pair) % 2

    def device(t, r):
        return (grp, t, r)

    fetch = pltpu.make_async_copy(w_ref, weight_in, weight_sem)
    fetch.start()

    barrier = pltpu.get_barrier_semaphore()
    me = tm * rows + row

    @pl.loop(1, 2 * rows)
    def _(step):
        other = lax.rem(me + step, 2 * rows)
        pl.semaphore_signal(
            barrier, inc=1, device_id=device(other // rows, other % rows),
            device_id_type=pl.DeviceIdType.MESH,
        )

    def half_of(array, slot, half):
        if array == 0:
            return act, pl.multiple_of((half + 1) * BLOCK, 16)
        return cot, pl.multiple_of(half * BLOCK, 16)

    def pack(array, slot, half, value):
        packed[array, slot, half, 0:BLOCK, :] = value[:, 0:128]
        packed[array, slot, half, BLOCK:PACKED, :] = jnp.concatenate(
            [value[0:WIDTH, 128:CH], value[WIDTH:BLOCK, 128:CH]], axis=1
        )

    def unpack(array, slot, half):
        ref, base = half_of(array, slot, half)
        ref[slot, pl.ds(base, BLOCK), 0:128] = packed[array, slot, half, 0:BLOCK, :]
        high = packed[array, slot, half, BLOCK:PACKED, :]
        ref[slot, pl.ds(base, WIDTH), 128:CH] = high[:, 0:64]
        ref[slot, pl.ds(pl.multiple_of(base + WIDTH, 16), WIDTH), 128:CH] = high[:, 64:128]

    def move(array, src_slot, dst_slot, half, lane, target):
        return pltpu.make_async_remote_copy(
            src_ref=packed.at[array, src_slot, half],
            dst_ref=packed.at[array, dst_slot, half],
            send_sem=send_sem.at[lane],
            recv_sem=recv_sem.at[array, dst_slot, half],
            device_id=target,
            device_id_type=pl.DeviceIdType.MESH,
        )

    def arrived(array, slot, half):
        move(array, slot, slot, half, 0, sibling).wait_recv()

    sibling = device(1 - tm, row)
    partner = device(tm, 2 * pair + 1 - side)
    outer_pair = pair + 2 * side - 1
    has_outer = jnp.logical_and(outer_pair >= 0, outer_pair < pairs)
    outer_same = device(tm, 2 * outer_pair + side)
    outer_cross = device(tm, 2 * outer_pair + 1 - side)
    outer_slot = 3 * (1 - side)
    cot_slot = 3 * side
    has_before, has_after = pair > 0, pair < pairs - 1

    inner_pair = pair + 1 - 2 * side
    has_same = jnp.logical_and(inner_pair >= 0, inner_pair < pairs)
    cross_slot, same_slot = cot_slot, outer_slot

    value = c_ref[...]
    cot[own, pl.ds(pl.multiple_of(tm * BLOCK, 16), BLOCK), :] = value
    pack(1, own, tm, value)
    pl.semaphore_wait(barrier, 2 * rows - 1)

    straight = [
        move(0, own, own, tm, 2, partner),
        move(1, own, own, tm, 3, partner),
        move(0, own, own, tm, 0, sibling),
        move(1, own, own, tm, 1, sibling),
    ]
    outward = [
        move(0, own, outer_slot, tm, 4, outer_cross),
        move(0, own, outer_slot, tm, 6, outer_same),
        move(1, own, outer_slot, tm, 5, outer_cross),
    ]
    straight[1].start()
    straight[3].start()
    x = x_ref[...].astype(f32)
    value = (x * (1.0 / (1.0 + jnp.exp(-x)))).astype(bf16)
    act[own, pl.ds(pl.multiple_of((tm + 1) * BLOCK, 16), BLOCK), :] = value
    pack(0, own, tm, value)
    straight[0].start()
    straight[2].start()

    @pl.when(has_outer)
    def _():
        outward[1].start()

    for slot in range(4):
        act[slot, 0:BLOCK, :] = jnp.zeros((BLOCK, CH), bf16)
        cot[slot, 2 * BLOCK : 3 * BLOCK, :] = jnp.zeros((BLOCK, CH), bf16)

    for slot, present in ((0, has_before), (3, has_after)):

        @pl.when(jnp.logical_not(present))
        def _():
            act[slot, BLOCK : 3 * BLOCK, :] = jnp.zeros((2 * BLOCK, CH), bf16)
            cot[slot, 0 : 2 * BLOCK, :] = jnp.zeros((2 * BLOCK, CH), bf16)

    pad[0:8, :] = jnp.zeros((8, CH), f32)
    pad[WIDTH + 8 : WIDTH + 16, :] = jnp.zeros((8, CH), f32)

    fetch.wait()
    for tap in range(TAPS):
        taps[tap] = weight_in[:, tap * CH : (tap + 1) * CH]

    def convolve(act_h, cot_h, first):
        @pl.loop(0, 3)
        def _(step_t):
            a = act[side + act_h, pl.ds(pl.multiple_of((2 * tm + step_t) * WIDTH, 16), BLOCK), :]
            c = cot[
                side + 2 - cot_h,
                pl.ds(pl.multiple_of((2 * tm + 2 - step_t) * WIDTH, 16), BLOCK),
                :,
            ]
            for step_w in range(3):
                y = lax.dot_general(
                    a,
                    taps[(step_t * 3 + act_h) * 3 + step_w],
                    (((1,), (1,)), ((), ())),
                    preferred_element_type=f32,
                )
                z = jnp.dot(
                    c, taps[(step_t * 3 + cot_h) * 3 + step_w], preferred_element_type=f32
                )
                if first:

                    @pl.when(step_t == 0)
                    def _():
                        fwd[step_w] = y
                        bwd[step_w] = z

                    @pl.when(step_t > 0)
                    def _():
                        fwd[step_w] += y
                        bwd[step_w] += z
                else:
                    fwd[step_w] += y
                    bwd[step_w] += z

    def shift(h):
        @pl.loop(0, 4)
        def _(frame):
            rows_of = pl.ds(pl.multiple_of(frame * WIDTH, 16), WIDTH)
            value = cot[1 + h, rows_of, :]
            pad[8 : WIDTH + 8, :] = value.astype(f32)
            shifted[0, h, rows_of, :] = pad[9 : WIDTH + 9, :].astype(bf16)
            shifted[1, h, rows_of, :] = value
            shifted[2, h, rows_of, :] = pad[7 : WIDTH + 7, :].astype(bf16)

    other_slot = 2 - side
    arrived(0, own, 1 - tm)
    unpack(0, own, 1 - tm)
    arrived(1, own, 1 - tm)
    unpack(1, own, 1 - tm)
    convolve(1, 1, True)
    shift(side)

    onward = [move(0, other_slot, other_slot, tm, 7, sibling), move(1, other_slot, other_slot, tm, 8, sibling)]
    same = move(0, same_slot, same_slot, tm, 9, sibling)
    cross = move(0, cross_slot, cross_slot, tm, 10, sibling)
    edge = move(1, cot_slot, cot_slot, tm, 11, sibling)
    for array in (1, 0):
        arrived(array, other_slot, tm)
        onward[array].start()

    @pl.when(has_outer)
    def _():
        outward[0].start()
        outward[2].start()

    @pl.when(has_same)
    def _():
        arrived(0, same_slot, tm)
        same.start()
        unpack(0, same_slot, tm)

    for array in range(2):
        unpack(array, other_slot, tm)
    for array in range(2):
        arrived(array, other_slot, 1 - tm)
        unpack(array, other_slot, 1 - tm)
    shift(1 - side)

    quarter = 2 * tm + window
    per_window = pairs * chunk
    held = filt.shape[0] // CH
    starts = [min(q * per_window // CH, TAPS - held) for q in range(4)]
    first_tap = jnp.int32(starts[0])
    for q in range(1, 4):
        first_tap = jnp.where(quarter == q, jnp.int32(starts[q]), first_tap)

    def filter_term(n, h, slot):
        tap = first_tap + n
        span = pl.ds(pl.multiple_of((tap // 9) * WIDTH, 16), 4 * WIDTH)
        return lax.dot_general(
            act[slot, span, :],
            shifted[tap % 3, h],
            (((0,), (0,)), ((), ())),
            preferred_element_type=f32,
        )

    def inner_rows(n):
        step_h = ((first_tap + n) // 3) % 3
        here = pl.ds(pl.multiple_of(n * CH, 16), CH)
        h = jnp.where(step_h == 0, 1, 0)
        filt[here, :] = filter_term(n, h, h + step_h)

        @pl.when(step_h == 1)
        def _():
            filt[here, :] += filter_term(n, 1, 2)

    def outer_rows(slot, n):
        step_h = ((first_tap + n) // 3) % 3
        here = pl.ds(pl.multiple_of(n * CH, 16), CH)

        @pl.when(step_h == jnp.where(slot == 0, 0, 2))
        def _():
            filt[here, :] += filter_term(n, slot // 3, slot)

    pl.loop(0, held)(inner_rows)

    @pl.when(has_same)
    def _():
        arrived(0, same_slot, 1 - tm)
        unpack(0, same_slot, 1 - tm)

    pl.loop(0, held)(functools.partial(outer_rows, same_slot))

    @pl.when(has_outer)
    def _():
        arrived(0, cross_slot, tm)
        cross.start()
        unpack(0, cross_slot, tm)
        arrived(0, cross_slot, 1 - tm)
        unpack(0, cross_slot, 1 - tm)

    pl.loop(0, held)(functools.partial(outer_rows, cross_slot))

    tall, cut = -(-chunk // 16) * 16, -(-chunk // 32) * 16
    for q in range(4):

        @pl.when(quarter == q)
        def _():
            for i in range(pairs):
                base = q * per_window - starts[q] * CH + i * chunk
                outgoing[i, 0:chunk, :] = filt[base : base + chunk, 0:128].astype(bf16)
                outgoing[i, tall : tall + cut, 0:64] = filt[base : base + cut, 128:CH].astype(bf16)
                outgoing[i, tall : tall + chunk - cut, 64:128] = filt[
                    base + cut : base + chunk, 128:CH
                ].astype(bf16)

    pieces = []
    for i in range(pairs):
        owner = window * pairs + i
        piece = pltpu.make_async_remote_copy(
            src_ref=outgoing.at[i],
            dst_ref=incoming.at[pair],
            send_sem=piece_send.at[i],
            recv_sem=piece_recv.at[pair],
            device_id=device(tm, owner),
            device_id_type=pl.DeviceIdType.MESH,
        )
        pieces.append((owner, piece))

        @pl.when(owner != row)
        def _():
            piece.start()

        @pl.when(owner == row)
        def _():
            incoming[pair] = outgoing[i]

    @pl.when(has_outer)
    def _():
        arrived(1, cot_slot, tm)
        edge.start()
        unpack(1, cot_slot, tm)

    convolve(2 - 2 * side, 2 * side, False)

    @pl.when(has_outer)
    def _():
        arrived(1, cot_slot, 1 - tm)
        unpack(1, cot_slot, 1 - tm)

    convolve(2 * side, 2 - 2 * side, False)

    for frame in range(2):
        span = pl.ds(frame * WIDTH, WIDTH)
        inner = pl.ds(8, WIDTH)
        pad[inner, :] = fwd[0, span, :]
        value = fwd[1, span, :] + pad[7 : WIDTH + 7, :]
        pad[inner, :] = fwd[2, span, :]
        value = value + pad[9 : WIDTH + 9, :]
        out_ref[span, :] = value.astype(bf16)
        pad[inner, :] = bwd[0, span, :]
        value = bwd[1, span, :] + pad[9 : WIDTH + 9, :]
        pad[inner, :] = bwd[2, span, :]
        value = value + pad[7 : WIDTH + 7, :]
        x = x_ref[span, :].astype(f32)
        sigma = 1.0 / (1.0 + jnp.exp(-x))
        ig_ref[span, :] = (value * sigma * (1.0 + x * (1.0 - sigma))).astype(bf16)

    for source in range(pairs):
        from_row = 2 * source + (row // pairs + source) % 2

        @pl.when(from_row != row)
        def _():
            pltpu.make_async_remote_copy(
                src_ref=outgoing.at[0],
                dst_ref=incoming.at[source],
                send_sem=piece_send.at[0],
                recv_sem=piece_recv.at[source],
                device_id=sibling,
                device_id_type=pl.DeviceIdType.MESH,
            ).wait_recv()

    total = incoming[0].astype(f32)
    for source in range(1, pairs):
        total = total + incoming[source].astype(f32)
    total = (total / scale).astype(bf16)
    fg_ref[:, 0:128] = total[0:chunk]
    fg_ref[0:cut, 128:CH] = total[tall : tall + cut, 0:64]
    fg_ref[cut:chunk, 128:CH] = total[tall : tall + chunk - cut, 64:128]

    for copy in straight + onward:
        copy.wait_send()

    @pl.when(has_outer)
    def _():
        for copy in outward:
            copy.wait_send()
        edge.wait_send()
        cross.wait_send()

    @pl.when(has_same)
    def _():
        same.wait_send()

    for owner, piece in pieces:

        @pl.when(owner != row)
        def _():
            piece.wait_send()


def fused(inputs, weight, cotangent):
    frames, rows = inputs.shape[:2]
    tm_size, row_size = lax.axis_size("tm"), lax.axis_size("row")
    pairs = row_size // 2
    chunk = TAPS * CH // (2 * row_size)
    scale = frames * tm_size * rows * row_size
    quarter_rows = pairs * chunk
    held = max(
        -(-(q + 1) * quarter_rows // CH) - q * quarter_rows // CH for q in range(4)
    )
    piece_rows = -(-chunk // 16) * 16 + -(-chunk // 32) * 16
    vmem = pl.BlockSpec(memory_space=pltpu.VMEM)
    bf16, f32 = jnp.bfloat16, jnp.float32
    out, ig, fg = pl.pallas_call(
        functools.partial(fused_kernel, pairs, chunk, float(scale)),
        out_shape=(
            jax.ShapeDtypeStruct((BLOCK, CH), bf16),
            jax.ShapeDtypeStruct((BLOCK, CH), bf16),
            jax.ShapeDtypeStruct((chunk, CH), bf16),
        ),
        in_specs=[vmem, pl.BlockSpec(memory_space=pltpu.HBM), vmem],
        out_specs=(vmem, vmem, vmem),
        scratch_shapes=[
            pltpu.VMEM((4, 3 * BLOCK, CH), bf16),
            pltpu.VMEM((4, 3 * BLOCK, CH), bf16),
            pltpu.VMEM((2, 4, 2, PACKED, 128), bf16),
            pltpu.VMEM((CH, TAPS * CH), bf16),
            pltpu.VMEM((TAPS, CH, CH), bf16),
            pltpu.VMEM((3, 2, 2 * BLOCK, CH), bf16),
            pltpu.VMEM((held * CH, CH), f32),
            pltpu.VMEM((pairs, piece_rows, 128), bf16),
            pltpu.VMEM((pairs, piece_rows, 128), bf16),
            pltpu.VMEM((3, BLOCK, CH), f32),
            pltpu.VMEM((3, BLOCK, CH), f32),
            pltpu.VMEM((WIDTH + 16, CH), f32),
            pltpu.SemaphoreType.DMA,
            pltpu.SemaphoreType.DMA((12,)),
            pltpu.SemaphoreType.DMA((2, 4, 2)),
            pltpu.SemaphoreType.DMA((pairs,)),
            pltpu.SemaphoreType.DMA((pairs,)),
        ],
        compiler_params=pltpu.CompilerParams(
            collective_id=0, has_side_effects=True, vmem_limit_bytes=48 * 1024 * 1024
        ),
    )(inputs.reshape(BLOCK, CH), weight.T, cotangent.reshape(BLOCK, CH))
    shape = (frames, rows, WIDTH * CH)
    return out.reshape(shape), ig.reshape(shape), fg.reshape(-1)


def passed_along(array, axis, by):
    length = lax.axis_size(axis)
    pairs = [(i, i + by) for i in range(length) if 0 <= i + by < length]
    return lax.ppermute(array, axis, pairs)


def with_halo(array, sides, width):
    for axis, dim in sides:
        size, length = (lax.axis_size(axis), array.shape[dim])
        up = [(i, (i + 1) % size) for i in range(size - 1)]
        down = [(j, i) for i, j in up]
        last = lax.slice_in_dim(array, length - width, length, axis=dim)
        first = lax.slice_in_dim(array, 0, width, axis=dim)
        before = lax.ppermute(last, axis, up)
        after = lax.ppermute(first, axis, down)
        array = jnp.concatenate([before, array, after], axis=dim)
    return array


def on_device(inputs, weight, cotangent):
    frames = inputs.shape[0]
    rows = inputs.shape[1]
    act = jax.nn.silu(inputs.astype(jnp.float32)).astype(jnp.bfloat16)
    earlier = passed_along(act, "tm", 1)
    extended = jnp.concatenate([earlier, act], 0)
    extended = with_halo(extended, (("row", 1),), 1)
    extended = extended.reshape(frames + 2, rows + 2, WIDTH, CH)
    act_pad = jnp.pad(extended, ((0, 0), (0, 0), (1, 1), (0, 0)))
    cot_four = cotangent.reshape(frames, rows, WIDTH, CH)
    cot_flat = cot_four.reshape(-1, CH)
    output = jnp.zeros((frames * rows * WIDTH, CH), jnp.float32)
    blocks = []
    for step_t in range(3):
        for step_h in range(3):
            for step_w in range(3):
                offset = ((step_t * 3 + step_h) * 3 + step_w) * CH
                kernel = weight[offset : offset + CH]
                piece = act_pad[
                    step_t : step_t + frames, step_h : step_h + rows, step_w : step_w + WIDTH
                ].reshape(-1, CH)
                output = output + jnp.dot(piece, kernel, preferred_element_type=jnp.float32)
                blocks.append(
                    lax.dot_general(
                        piece,
                        cot_flat,
                        (((0,), (0,)), ((), ())),
                        preferred_element_type=jnp.float32,
                    )
                )
    spread = jnp.zeros((frames + 2, rows + 2, WIDTH + 2, CH), jnp.float32)
    for step_t in range(3):
        slab_weight = weight[step_t * 9 * CH : (step_t + 1) * 9 * CH]
        terms = lax.dot_general(
            cot_flat, slab_weight, (((1,), (1,)), ((), ())), preferred_element_type=jnp.float32
        )
        terms = terms.reshape(frames, rows, WIDTH, 9, CH)
        slab = jnp.zeros((frames, rows + 2, WIDTH + 2, CH), jnp.float32)
        for step_h in range(3):
            for step_w in range(3):
                slab = slab + jnp.pad(
                    terms[:, :, :, step_h * 3 + step_w],
                    ((0, 0), (step_h, 2 - step_h), (step_w, 2 - step_w), (0, 0)),
                )
        spread = spread + jnp.pad(slab, ((step_t, 2 - step_t), (0, 0), (0, 0), (0, 0)))
    inner = spread[:, :, 1 : WIDTH + 1]
    from_next = passed_along(inner[:, 0:1], "row", -1)
    from_prev = passed_along(inner[:, rows + 1 : rows + 2], "row", 1)
    center = inner[:, 1 : rows + 1]
    center = center.at[:, rows - 1 : rows].add(from_next)
    center = center.at[:, 0:1].add(from_prev)
    returned = passed_along(center[0:2], "tm", -1)
    grad_act = center[2:].at[frames - 2 :].add(returned).reshape(-1, CH)
    x_float = inputs.reshape(-1, CH).astype(jnp.float32)
    sigma = jax.nn.sigmoid(x_float)
    input_grad = (grad_act * sigma * (1.0 + x_float * (1.0 - sigma))).astype(jnp.bfloat16)
    local_filter = jnp.concatenate(blocks, 0).reshape(-1)
    frame_blocks = lax.axis_size("tm")
    row_blocks = lax.axis_size("row")
    scale = frames * frame_blocks * rows * row_blocks
    share = lax.psum_scatter(local_filter, ("tm", "row"), scatter_dimension=0, tiled=True)
    filter_grad = (share / scale).astype(jnp.bfloat16)
    shape = (frames, rows, WIDTH * CH)
    return (output.astype(jnp.bfloat16).reshape(shape), input_grad.reshape(shape), filter_grad)


def either(mesh, inputs, weight, cotangent):
    size = mesh.shape["row"]
    quads = mesh.shape["tm"] == 2 and size % 2 == 0 and TAPS * CH % (4 * size) == 0
    if quads and inputs.shape[:2] == (2, 1):
        return fused(inputs, weight, cotangent)
    return on_device(inputs, weight, cotangent)


def solution(mesh):
    placed = (P(("grp", "tm"), "row", None), P(), P(("grp", "tm"), "row", None))
    return jax.shard_map(
        functools.partial(either, mesh),
        mesh=mesh,
        in_specs=placed,
        out_specs=(
            P(("grp", "tm"), "row", None),
            P(("grp", "tm"), "row", None),
            P(("grp", "tm", "row")),
        ),
        check_vma=False,
    )
```

```python
import functools

import jax
import jax.numpy as jnp
from jax import lax
from jax.experimental import pallas as pl
from jax.experimental.pallas import tpu as pltpu
from jax.sharding import PartitionSpec as P

CH = 192
WIDTH = 224
TAPS = 27
BLOCK = 2 * WIDTH
PACKED = 3 * WIDTH


def fused_kernel(
    pairs, chunk, scale, x_ref, w_ref, c_ref, out_ref, ig_ref, fg_ref,
    act, cot, packed, weight_in, taps, shifted, filt, outgoing, incoming, fwd, bwd, pad,
    weight_sem, send_sem, recv_sem, piece_send, piece_recv,
):
    f32, bf16 = jnp.float32, jnp.bfloat16
    grp, tm, row = lax.axis_index("grp"), lax.axis_index("tm"), lax.axis_index("row")
    rows = 2 * pairs
    pair, side = row // 2, row % 2
    own = 1 + side
    window = (side + pair) % 2

    def device(t, r):
        return (grp, t, r)

    fetch = pltpu.make_async_copy(w_ref, weight_in, weight_sem)
    fetch.start()

    barrier = pltpu.get_barrier_semaphore()
    me = tm * rows + row

    @pl.loop(1, 2 * rows)
    def _(step):
        other = lax.rem(me + step, 2 * rows)
        pl.semaphore_signal(
            barrier, inc=1, device_id=device(other // rows, other % rows),
            device_id_type=pl.DeviceIdType.MESH,
        )

    def half_of(array, slot, half):
        if array == 0:
            return act, pl.multiple_of((half + 1) * BLOCK, 16)
        return cot, pl.multiple_of(half * BLOCK, 16)

    def pack(array, slot, half, value):
        packed[array, slot, half, 0:BLOCK, :] = value[:, 0:128]
        packed[array, slot, half, BLOCK:PACKED, :] = jnp.concatenate(
            [value[0:WIDTH, 128:CH], value[WIDTH:BLOCK, 128:CH]], axis=1
        )

    def unpack(array, slot, half):
        ref, base = half_of(array, slot, half)
        ref[slot, pl.ds(base, BLOCK), 0:128] = packed[array, slot, half, 0:BLOCK, :]
        high = packed[array, slot, half, BLOCK:PACKED, :]
        ref[slot, pl.ds(base, WIDTH), 128:CH] = high[:, 0:64]
        ref[slot, pl.ds(pl.multiple_of(base + WIDTH, 16), WIDTH), 128:CH] = high[:, 64:128]

    def move(array, src_slot, dst_slot, half, lane, target):
        return pltpu.make_async_remote_copy(
            src_ref=packed.at[array, src_slot, half],
            dst_ref=packed.at[array, dst_slot, half],
            send_sem=send_sem.at[lane],
            recv_sem=recv_sem.at[array, dst_slot, half],
            device_id=target,
            device_id_type=pl.DeviceIdType.MESH,
        )

    def arrived(array, slot, half):
        move(array, slot, slot, half, 0, sibling).wait_recv()

    sibling = device(1 - tm, row)
    partner = device(tm, 2 * pair + 1 - side)
    outer_pair = pair + 2 * side - 1
    has_outer = jnp.logical_and(outer_pair >= 0, outer_pair < pairs)
    outer_same = device(tm, 2 * outer_pair + side)
    outer_cross = device(tm, 2 * outer_pair + 1 - side)
    outer_slot = 3 * (1 - side)
    cot_slot = 3 * side
    has_before, has_after = pair > 0, pair < pairs - 1

    inner_pair = pair + 1 - 2 * side
    has_same = jnp.logical_and(inner_pair >= 0, inner_pair < pairs)
    cross_slot, same_slot = cot_slot, outer_slot

    value = c_ref[...]
    cot[own, pl.ds(pl.multiple_of(tm * BLOCK, 16), BLOCK), :] = value
    pack(1, own, tm, value)
    pl.semaphore_wait(barrier, 2 * rows - 1)

    straight = [
        move(0, own, own, tm, 2, partner),
        move(1, own, own, tm, 3, partner),
        move(0, own, own, tm, 0, sibling),
        move(1, own, own, tm, 1, sibling),
    ]
    outward = [
        move(0, own, outer_slot, tm, 4, outer_cross),
        move(0, own, outer_slot, tm, 6, outer_same),
        move(1, own, outer_slot, tm, 5, outer_cross),
    ]
    straight[1].start()
    straight[3].start()
    x = x_ref[...].astype(f32)
    value = (x * (1.0 / (1.0 + jnp.exp(-x)))).astype(bf16)
    act[own, pl.ds(pl.multiple_of((tm + 1) * BLOCK, 16), BLOCK), :] = value
    pack(0, own, tm, value)
    straight[0].start()
    straight[2].start()

    @pl.when(has_outer)
    def _():
        outward[1].start()

    for slot in range(4):
        act[slot, 0:BLOCK, :] = jnp.zeros((BLOCK, CH), bf16)
        cot[slot, 2 * BLOCK : 3 * BLOCK, :] = jnp.zeros((BLOCK, CH), bf16)

    for slot, present in ((0, has_before), (3, has_after)):

        @pl.when(jnp.logical_not(present))
        def _():
            act[slot, BLOCK : 3 * BLOCK, :] = jnp.zeros((2 * BLOCK, CH), bf16)
            cot[slot, 0 : 2 * BLOCK, :] = jnp.zeros((2 * BLOCK, CH), bf16)

    pad[0:8, :] = jnp.zeros((8, CH), f32)
    pad[WIDTH + 8 : WIDTH + 16, :] = jnp.zeros((8, CH), f32)

    fetch.wait()
    for tap in range(TAPS):
        taps[tap] = weight_in[:, tap * CH : (tap + 1) * CH]

    def convolve(act_h, cot_h, first):
        @pl.loop(0, 3)
        def _(step_t):
            a = act[side + act_h, pl.ds(pl.multiple_of((2 * tm + step_t) * WIDTH, 16), BLOCK), :]
            c = cot[
                side + 2 - cot_h,
                pl.ds(pl.multiple_of((2 * tm + 2 - step_t) * WIDTH, 16), BLOCK),
                :,
            ]
            for step_w in range(3):
                y = lax.dot_general(
                    a,
                    taps[(step_t * 3 + act_h) * 3 + step_w],
                    (((1,), (1,)), ((), ())),
                    preferred_element_type=f32,
                )
                z = jnp.dot(
                    c, taps[(step_t * 3 + cot_h) * 3 + step_w], preferred_element_type=f32
                )
                if first:

                    @pl.when(step_t == 0)
                    def _():
                        fwd[step_w] = y
                        bwd[step_w] = z

                    @pl.when(step_t > 0)
                    def _():
                        fwd[step_w] += y
                        bwd[step_w] += z
                else:
                    fwd[step_w] += y
                    bwd[step_w] += z

    def shift(h):
        @pl.loop(0, 4)
        def _(frame):
            rows_of = pl.ds(pl.multiple_of(frame * WIDTH, 16), WIDTH)
            value = cot[1 + h, rows_of, :]
            pad[8 : WIDTH + 8, :] = value.astype(f32)
            shifted[0, h, rows_of, :] = pad[9 : WIDTH + 9, :].astype(bf16)
            shifted[1, h, rows_of, :] = value
            shifted[2, h, rows_of, :] = pad[7 : WIDTH + 7, :].astype(bf16)

    other_slot = 2 - side
    arrived(0, own, 1 - tm)
    unpack(0, own, 1 - tm)
    arrived(1, own, 1 - tm)
    unpack(1, own, 1 - tm)
    convolve(1, 1, True)
    shift(side)

    onward = [move(0, other_slot, other_slot, tm, 7, sibling), move(1, other_slot, other_slot, tm, 8, sibling)]
    same = move(0, same_slot, same_slot, tm, 9, sibling)
    cross = move(0, cross_slot, cross_slot, tm, 10, sibling)
    edge = move(1, cot_slot, cot_slot, tm, 11, sibling)
    for array in (1, 0):
        arrived(array, other_slot, tm)
        onward[array].start()

    @pl.when(has_outer)
    def _():
        outward[0].start()
        outward[2].start()

    @pl.when(has_same)
    def _():
        arrived(0, same_slot, tm)
        same.start()
        unpack(0, same_slot, tm)

    for array in range(2):
        unpack(array, other_slot, tm)
    for array in range(2):
        arrived(array, other_slot, 1 - tm)
        unpack(array, other_slot, 1 - tm)
    shift(1 - side)

    quarter = 2 * tm + window
    per_window = pairs * chunk
    held = filt.shape[0] // CH
    starts = [min(q * per_window // CH, TAPS - held) for q in range(4)]
    first_tap = jnp.int32(starts[0])
    for q in range(1, 4):
        first_tap = jnp.where(quarter == q, jnp.int32(starts[q]), first_tap)

    def filter_term(n, h, slot):
        tap = first_tap + n
        span = pl.ds(pl.multiple_of((tap // 9) * WIDTH, 16), 4 * WIDTH)
        return lax.dot_general(
            act[slot, span, :],
            shifted[tap % 3, h],
            (((0,), (0,)), ((), ())),
            preferred_element_type=f32,
        )

    def inner_rows(n):
        step_h = ((first_tap + n) // 3) % 3
        here = pl.ds(pl.multiple_of(n * CH, 16), CH)
        h = jnp.where(step_h == 0, 1, 0)
        filt[here, :] = filter_term(n, h, h + step_h)

        @pl.when(step_h == 1)
        def _():
            filt[here, :] += filter_term(n, 1, 2)

    def outer_rows(slot, n):
        step_h = ((first_tap + n) // 3) % 3
        here = pl.ds(pl.multiple_of(n * CH, 16), CH)

        @pl.when(step_h == jnp.where(slot == 0, 0, 2))
        def _():
            filt[here, :] += filter_term(n, slot // 3, slot)

    pl.loop(0, held)(inner_rows)

    @pl.when(has_same)
    def _():
        arrived(0, same_slot, 1 - tm)
        unpack(0, same_slot, 1 - tm)

    pl.loop(0, held)(functools.partial(outer_rows, same_slot))

    @pl.when(has_outer)
    def _():
        arrived(0, cross_slot, tm)
        cross.start()
        unpack(0, cross_slot, tm)
        arrived(0, cross_slot, 1 - tm)
        unpack(0, cross_slot, 1 - tm)

    pl.loop(0, held)(functools.partial(outer_rows, cross_slot))

    pieces = []
    for i in range(pairs):
        owner = window * pairs + i
        piece = pltpu.make_async_remote_copy(
            src_ref=outgoing.at[i],
            dst_ref=incoming.at[pair],
            send_sem=piece_send.at[i],
            recv_sem=piece_recv.at[pair],
            device_id=device(tm, owner),
            device_id_type=pl.DeviceIdType.MESH,
        )
        pieces.append((owner, piece))

    tall, cut = -(-chunk // 16) * 16, -(-chunk // 32) * 16
    for q in range(4):

        @pl.when(quarter == q)
        def _():
            for i in range(pairs):
                base = q * per_window - starts[q] * CH + i * chunk
                outgoing[i, 0:chunk, :] = filt[base : base + chunk, 0:128].astype(bf16)
                outgoing[i, tall : tall + cut, 0:64] = filt[base : base + cut, 128:CH].astype(bf16)
                outgoing[i, tall : tall + chunk - cut, 64:128] = filt[
                    base + cut : base + chunk, 128:CH
                ].astype(bf16)
                owner, piece = pieces[i]

                @pl.when(owner != row)
                def _():
                    piece.start()

                @pl.when(owner == row)
                def _():
                    incoming[pair] = outgoing[i]

    @pl.when(has_outer)
    def _():
        arrived(1, cot_slot, tm)
        edge.start()
        unpack(1, cot_slot, tm)

    convolve(2 - 2 * side, 2 * side, False)

    @pl.when(has_outer)
    def _():
        arrived(1, cot_slot, 1 - tm)
        unpack(1, cot_slot, 1 - tm)

    convolve(2 * side, 2 - 2 * side, False)

    for frame in range(2):
        span = pl.ds(frame * WIDTH, WIDTH)
        inner = pl.ds(8, WIDTH)
        pad[inner, :] = fwd[0, span, :]
        value = fwd[1, span, :] + pad[7 : WIDTH + 7, :]
        pad[inner, :] = fwd[2, span, :]
        value = value + pad[9 : WIDTH + 9, :]
        out_ref[span, :] = value.astype(bf16)
        pad[inner, :] = bwd[0, span, :]
        value = bwd[1, span, :] + pad[9 : WIDTH + 9, :]
        pad[inner, :] = bwd[2, span, :]
        value = value + pad[7 : WIDTH + 7, :]
        x = x_ref[span, :].astype(f32)
        sigma = 1.0 / (1.0 + jnp.exp(-x))
        ig_ref[span, :] = (value * sigma * (1.0 + x * (1.0 - sigma))).astype(bf16)

    for source in range(pairs):
        from_row = 2 * source + (row // pairs + source) % 2

        @pl.when(from_row != row)
        def _():
            pltpu.make_async_remote_copy(
                src_ref=outgoing.at[0],
                dst_ref=incoming.at[source],
                send_sem=piece_send.at[0],
                recv_sem=piece_recv.at[source],
                device_id=sibling,
                device_id_type=pl.DeviceIdType.MESH,
            ).wait_recv()

    total = incoming[0].astype(f32)
    for source in range(1, pairs):
        total = total + incoming[source].astype(f32)
    total = (total / scale).astype(bf16)
    fg_ref[:, 0:128] = total[0:chunk]
    fg_ref[0:cut, 128:CH] = total[tall : tall + cut, 0:64]
    fg_ref[cut:chunk, 128:CH] = total[tall : tall + chunk - cut, 64:128]

    for copy in straight + onward:
        copy.wait_send()

    @pl.when(has_outer)
    def _():
        for copy in outward:
            copy.wait_send()
        edge.wait_send()
        cross.wait_send()

    @pl.when(has_same)
    def _():
        same.wait_send()

    for owner, piece in pieces:

        @pl.when(owner != row)
        def _():
            piece.wait_send()


def fused(inputs, weight, cotangent):
    frames, rows = inputs.shape[:2]
    tm_size, row_size = lax.axis_size("tm"), lax.axis_size("row")
    pairs = row_size // 2
    chunk = TAPS * CH // (2 * row_size)
    scale = frames * tm_size * rows * row_size
    quarter_rows = pairs * chunk
    held = max(
        -(-(q + 1) * quarter_rows // CH) - q * quarter_rows // CH for q in range(4)
    )
    piece_rows = -(-chunk // 16) * 16 + -(-chunk // 32) * 16
    vmem = pl.BlockSpec(memory_space=pltpu.VMEM)
    bf16, f32 = jnp.bfloat16, jnp.float32
    out, ig, fg = pl.pallas_call(
        functools.partial(fused_kernel, pairs, chunk, float(scale)),
        out_shape=(
            jax.ShapeDtypeStruct((BLOCK, CH), bf16),
            jax.ShapeDtypeStruct((BLOCK, CH), bf16),
            jax.ShapeDtypeStruct((chunk, CH), bf16),
        ),
        in_specs=[vmem, pl.BlockSpec(memory_space=pltpu.HBM), vmem],
        out_specs=(vmem, vmem, vmem),
        scratch_shapes=[
            pltpu.VMEM((4, 3 * BLOCK, CH), bf16),
            pltpu.VMEM((4, 3 * BLOCK, CH), bf16),
            pltpu.VMEM((2, 4, 2, PACKED, 128), bf16),
            pltpu.VMEM((CH, TAPS * CH), bf16),
            pltpu.VMEM((TAPS, CH, CH), bf16),
            pltpu.VMEM((3, 2, 2 * BLOCK, CH), bf16),
            pltpu.VMEM((held * CH, CH), f32),
            pltpu.VMEM((pairs, piece_rows, 128), bf16),
            pltpu.VMEM((pairs, piece_rows, 128), bf16),
            pltpu.VMEM((3, BLOCK, CH), f32),
            pltpu.VMEM((3, BLOCK, CH), f32),
            pltpu.VMEM((WIDTH + 16, CH), f32),
            pltpu.SemaphoreType.DMA,
            pltpu.SemaphoreType.DMA((12,)),
            pltpu.SemaphoreType.DMA((2, 4, 2)),
            pltpu.SemaphoreType.DMA((pairs,)),
            pltpu.SemaphoreType.DMA((pairs,)),
        ],
        compiler_params=pltpu.CompilerParams(
            collective_id=0, has_side_effects=True, vmem_limit_bytes=48 * 1024 * 1024
        ),
    )(inputs.reshape(BLOCK, CH), weight.T, cotangent.reshape(BLOCK, CH))
    shape = (frames, rows, WIDTH * CH)
    return out.reshape(shape), ig.reshape(shape), fg.reshape(-1)


def passed_along(array, axis, by):
    length = lax.axis_size(axis)
    pairs = [(i, i + by) for i in range(length) if 0 <= i + by < length]
    return lax.ppermute(array, axis, pairs)


def with_halo(array, sides, width):
    for axis, dim in sides:
        size, length = (lax.axis_size(axis), array.shape[dim])
        up = [(i, (i + 1) % size) for i in range(size - 1)]
        down = [(j, i) for i, j in up]
        last = lax.slice_in_dim(array, length - width, length, axis=dim)
        first = lax.slice_in_dim(array, 0, width, axis=dim)
        before = lax.ppermute(last, axis, up)
        after = lax.ppermute(first, axis, down)
        array = jnp.concatenate([before, array, after], axis=dim)
    return array


def on_device(inputs, weight, cotangent):
    frames = inputs.shape[0]
    rows = inputs.shape[1]
    act = jax.nn.silu(inputs.astype(jnp.float32)).astype(jnp.bfloat16)
    earlier = passed_along(act, "tm", 1)
    extended = jnp.concatenate([earlier, act], 0)
    extended = with_halo(extended, (("row", 1),), 1)
    extended = extended.reshape(frames + 2, rows + 2, WIDTH, CH)
    act_pad = jnp.pad(extended, ((0, 0), (0, 0), (1, 1), (0, 0)))
    cot_four = cotangent.reshape(frames, rows, WIDTH, CH)
    cot_flat = cot_four.reshape(-1, CH)
    output = jnp.zeros((frames * rows * WIDTH, CH), jnp.float32)
    blocks = []
    for step_t in range(3):
        for step_h in range(3):
            for step_w in range(3):
                offset = ((step_t * 3 + step_h) * 3 + step_w) * CH
                kernel = weight[offset : offset + CH]
                piece = act_pad[
                    step_t : step_t + frames, step_h : step_h + rows, step_w : step_w + WIDTH
                ].reshape(-1, CH)
                output = output + jnp.dot(piece, kernel, preferred_element_type=jnp.float32)
                blocks.append(
                    lax.dot_general(
                        piece,
                        cot_flat,
                        (((0,), (0,)), ((), ())),
                        preferred_element_type=jnp.float32,
                    )
                )
    spread = jnp.zeros((frames + 2, rows + 2, WIDTH + 2, CH), jnp.float32)
    for step_t in range(3):
        slab_weight = weight[step_t * 9 * CH : (step_t + 1) * 9 * CH]
        terms = lax.dot_general(
            cot_flat, slab_weight, (((1,), (1,)), ((), ())), preferred_element_type=jnp.float32
        )
        terms = terms.reshape(frames, rows, WIDTH, 9, CH)
        slab = jnp.zeros((frames, rows + 2, WIDTH + 2, CH), jnp.float32)
        for step_h in range(3):
            for step_w in range(3):
                slab = slab + jnp.pad(
                    terms[:, :, :, step_h * 3 + step_w],
                    ((0, 0), (step_h, 2 - step_h), (step_w, 2 - step_w), (0, 0)),
                )
        spread = spread + jnp.pad(slab, ((step_t, 2 - step_t), (0, 0), (0, 0), (0, 0)))
    inner = spread[:, :, 1 : WIDTH + 1]
    from_next = passed_along(inner[:, 0:1], "row", -1)
    from_prev = passed_along(inner[:, rows + 1 : rows + 2], "row", 1)
    center = inner[:, 1 : rows + 1]
    center = center.at[:, rows - 1 : rows].add(from_next)
    center = center.at[:, 0:1].add(from_prev)
    returned = passed_along(center[0:2], "tm", -1)
    grad_act = center[2:].at[frames - 2 :].add(returned).reshape(-1, CH)
    x_float = inputs.reshape(-1, CH).astype(jnp.float32)
    sigma = jax.nn.sigmoid(x_float)
    input_grad = (grad_act * sigma * (1.0 + x_float * (1.0 - sigma))).astype(jnp.bfloat16)
    local_filter = jnp.concatenate(blocks, 0).reshape(-1)
    frame_blocks = lax.axis_size("tm")
    row_blocks = lax.axis_size("row")
    scale = frames * frame_blocks * rows * row_blocks
    share = lax.psum_scatter(local_filter, ("tm", "row"), scatter_dimension=0, tiled=True)
    filter_grad = (share / scale).astype(jnp.bfloat16)
    shape = (frames, rows, WIDTH * CH)
    return (output.astype(jnp.bfloat16).reshape(shape), input_grad.reshape(shape), filter_grad)


def either(mesh, inputs, weight, cotangent):
    size = mesh.shape["row"]
    quads = mesh.shape["tm"] == 2 and size % 2 == 0 and TAPS * CH % (4 * size) == 0
    if quads and inputs.shape[:2] == (2, 1):
        return fused(inputs, weight, cotangent)
    return on_device(inputs, weight, cotangent)


def solution(mesh):
    placed = (P(("grp", "tm"), "row", None), P(), P(("grp", "tm"), "row", None))
    return jax.shard_map(
        functools.partial(either, mesh),
        mesh=mesh,
        in_specs=placed,
        out_specs=(
            P(("grp", "tm"), "row", None),
            P(("grp", "tm"), "row", None),
            P(("grp", "tm", "row")),
        ),
        check_vma=False,
    )
```

```python
import functools

import jax
import jax.numpy as jnp
from jax import lax
from jax.experimental import pallas as pl
from jax.experimental.pallas import tpu as pltpu
from jax.sharding import PartitionSpec as P

CH = 192
WIDTH = 224
TAPS = 27
BLOCK = 2 * WIDTH
PACKED = 3 * WIDTH


def fused_kernel(
    pairs, chunk, scale, x_ref, w_ref, c_ref, out_ref, ig_ref, fg_ref,
    act, cot, packed, weight_in, taps, shifted, filt, outgoing, incoming, fwd, bwd, pad,
    weight_sem, send_sem, recv_sem, piece_send, piece_recv,
):
    f32, bf16 = jnp.float32, jnp.bfloat16
    grp, tm, row = lax.axis_index("grp"), lax.axis_index("tm"), lax.axis_index("row")
    rows = 2 * pairs
    pair, side = row // 2, row % 2
    own = 1 + side
    window = (side + pair) % 2

    def device(t, r):
        return (grp, t, r)

    fetch = pltpu.make_async_copy(w_ref, weight_in, weight_sem)
    fetch.start()

    barrier = pltpu.get_barrier_semaphore()
    me = tm * rows + row

    @pl.loop(1, 2 * rows)
    def _(step):
        other = lax.rem(me + step, 2 * rows)
        pl.semaphore_signal(
            barrier, inc=1, device_id=device(other // rows, other % rows),
            device_id_type=pl.DeviceIdType.MESH,
        )

    def half_of(array, slot, half):
        if array == 0:
            return act, pl.multiple_of((half + 1) * BLOCK, 16)
        return cot, pl.multiple_of(half * BLOCK, 16)

    def pack(array, slot, half, value):
        packed[array, slot, half, 0:BLOCK, :] = value[:, 0:128]
        packed[array, slot, half, BLOCK:PACKED, :] = jnp.concatenate(
            [value[0:WIDTH, 128:CH], value[WIDTH:BLOCK, 128:CH]], axis=1
        )

    def unpack(array, slot, half):
        ref, base = half_of(array, slot, half)
        ref[slot, pl.ds(base, BLOCK), 0:128] = packed[array, slot, half, 0:BLOCK, :]
        high = packed[array, slot, half, BLOCK:PACKED, :]
        ref[slot, pl.ds(base, WIDTH), 128:CH] = high[:, 0:64]
        ref[slot, pl.ds(pl.multiple_of(base + WIDTH, 16), WIDTH), 128:CH] = high[:, 64:128]

    def move(array, src_slot, dst_slot, half, lane, target):
        return pltpu.make_async_remote_copy(
            src_ref=packed.at[array, src_slot, half],
            dst_ref=packed.at[array, dst_slot, half],
            send_sem=send_sem.at[lane],
            recv_sem=recv_sem.at[array, dst_slot, half],
            device_id=target,
            device_id_type=pl.DeviceIdType.MESH,
        )

    def arrived(array, slot, half):
        move(array, slot, slot, half, 0, sibling).wait_recv()

    sibling = device(1 - tm, row)
    partner = device(tm, 2 * pair + 1 - side)
    outer_pair = pair + 2 * side - 1
    has_outer = jnp.logical_and(outer_pair >= 0, outer_pair < pairs)
    outer_same = device(tm, 2 * outer_pair + side)
    outer_cross = device(tm, 2 * outer_pair + 1 - side)
    outer_slot = 3 * (1 - side)
    cot_slot = 3 * side
    has_before, has_after = pair > 0, pair < pairs - 1

    inner_pair = pair + 1 - 2 * side
    has_same = jnp.logical_and(inner_pair >= 0, inner_pair < pairs)
    cross_slot, same_slot = cot_slot, outer_slot

    value = c_ref[...]
    cot[own, pl.ds(pl.multiple_of(tm * BLOCK, 16), BLOCK), :] = value
    pack(1, own, tm, value)
    pl.semaphore_wait(barrier, 2 * rows - 1)

    straight = [
        move(0, own, own, tm, 2, partner),
        move(1, own, own, tm, 3, partner),
        move(0, own, own, tm, 0, sibling),
        move(1, own, own, tm, 1, sibling),
    ]
    outward = [
        move(0, own, outer_slot, tm, 4, outer_cross),
        move(0, own, outer_slot, tm, 6, outer_same),
        move(1, own, outer_slot, tm, 5, outer_cross),
    ]
    straight[1].start()
    straight[3].start()
    x = x_ref[...].astype(f32)
    value = (x * (1.0 / (1.0 + jnp.exp(-x)))).astype(bf16)
    act[own, pl.ds(pl.multiple_of((tm + 1) * BLOCK, 16), BLOCK), :] = value
    pack(0, own, tm, value)
    straight[0].start()
    straight[2].start()

    @pl.when(has_outer)
    def _():
        outward[1].start()

    for slot in range(4):
        act[slot, 0:BLOCK, :] = jnp.zeros((BLOCK, CH), bf16)
        cot[slot, 2 * BLOCK : 3 * BLOCK, :] = jnp.zeros((BLOCK, CH), bf16)

    for slot, present in ((0, has_before), (3, has_after)):

        @pl.when(jnp.logical_not(present))
        def _():
            act[slot, BLOCK : 3 * BLOCK, :] = jnp.zeros((2 * BLOCK, CH), bf16)
            cot[slot, 0 : 2 * BLOCK, :] = jnp.zeros((2 * BLOCK, CH), bf16)

    pad[0:8, :] = jnp.zeros((8, CH), f32)
    pad[WIDTH + 8 : WIDTH + 16, :] = jnp.zeros((8, CH), f32)

    fetch.wait()
    for tap in range(TAPS):
        taps[tap] = weight_in[:, tap * CH : (tap + 1) * CH]

    def convolve(act_h, cot_h, first):
        @pl.loop(0, 3)
        def _(step_t):
            a = act[side + act_h, pl.ds(pl.multiple_of((2 * tm + step_t) * WIDTH, 16), BLOCK), :]
            c = cot[
                side + 2 - cot_h,
                pl.ds(pl.multiple_of((2 * tm + 2 - step_t) * WIDTH, 16), BLOCK),
                :,
            ]
            for step_w in range(3):
                y = lax.dot_general(
                    a,
                    taps[(step_t * 3 + act_h) * 3 + step_w],
                    (((1,), (1,)), ((), ())),
                    preferred_element_type=f32,
                )
                z = jnp.dot(
                    c, taps[(step_t * 3 + cot_h) * 3 + step_w], preferred_element_type=f32
                )
                if first:

                    @pl.when(step_t == 0)
                    def _():
                        fwd[step_w] = y
                        bwd[step_w] = z

                    @pl.when(step_t > 0)
                    def _():
                        fwd[step_w] += y
                        bwd[step_w] += z
                else:
                    fwd[step_w] += y
                    bwd[step_w] += z

    def shift(h):
        @pl.loop(0, 4)
        def _(frame):
            rows_of = pl.ds(pl.multiple_of(frame * WIDTH, 16), WIDTH)
            value = cot[1 + h, rows_of, :]
            pad[8 : WIDTH + 8, :] = value.astype(f32)
            shifted[0, h, rows_of, :] = pad[9 : WIDTH + 9, :].astype(bf16)
            shifted[1, h, rows_of, :] = value
            shifted[2, h, rows_of, :] = pad[7 : WIDTH + 7, :].astype(bf16)

    other_slot = 2 - side
    arrived(0, own, 1 - tm)
    unpack(0, own, 1 - tm)
    arrived(1, own, 1 - tm)
    unpack(1, own, 1 - tm)
    convolve(1, 1, True)
    shift(side)

    onward = [move(0, other_slot, other_slot, tm, 7, sibling), move(1, other_slot, other_slot, tm, 8, sibling)]
    same = move(0, same_slot, same_slot, tm, 9, sibling)
    cross = move(0, cross_slot, cross_slot, tm, 10, sibling)
    edge = move(1, cot_slot, cot_slot, tm, 11, sibling)
    for array in (1, 0):
        arrived(array, other_slot, tm)
        onward[array].start()

    @pl.when(has_outer)
    def _():
        outward[0].start()
        outward[2].start()

    @pl.when(has_same)
    def _():
        arrived(0, same_slot, tm)
        same.start()
        unpack(0, same_slot, tm)

    for array in range(2):
        unpack(array, other_slot, tm)
    for array in range(2):
        arrived(array, other_slot, 1 - tm)
        unpack(array, other_slot, 1 - tm)
    shift(1 - side)

    quarter = 2 * tm + window
    per_window = pairs * chunk
    held = filt.shape[0] // CH
    starts = [min(q * per_window // CH, TAPS - held) for q in range(4)]
    first_tap = jnp.int32(starts[0])
    for q in range(1, 4):
        first_tap = jnp.where(quarter == q, jnp.int32(starts[q]), first_tap)

    def filter_term(n, h, slot):
        tap = first_tap + n
        span = pl.ds(pl.multiple_of((tap // 9) * WIDTH, 16), 4 * WIDTH)
        return lax.dot_general(
            act[slot, span, :],
            shifted[tap % 3, h],
            (((0,), (0,)), ((), ())),
            preferred_element_type=f32,
        )

    def inner_rows(n):
        step_h = ((first_tap + n) // 3) % 3
        here = pl.ds(pl.multiple_of(n * CH, 16), CH)
        h = jnp.where(step_h == 0, 1, 0)
        filt[here, :] = filter_term(n, h, h + step_h)

        @pl.when(step_h == 1)
        def _():
            filt[here, :] += filter_term(n, 1, 2)

    def outer_rows(slot, n):
        step_h = ((first_tap + n) // 3) % 3
        here = pl.ds(pl.multiple_of(n * CH, 16), CH)

        @pl.when(step_h == jnp.where(slot == 0, 0, 2))
        def _():
            filt[here, :] += filter_term(n, slot // 3, slot)

    pl.loop(0, held)(inner_rows)

    @pl.when(has_same)
    def _():
        arrived(0, same_slot, 1 - tm)
        unpack(0, same_slot, 1 - tm)

    pl.loop(0, held)(functools.partial(outer_rows, same_slot))

    @pl.when(has_outer)
    def _():
        arrived(0, cross_slot, tm)
        cross.start()
        unpack(0, cross_slot, tm)

    convolve(2 - 2 * side, 2 * side, False)

    @pl.when(has_outer)
    def _():
        arrived(0, cross_slot, 1 - tm)
        unpack(0, cross_slot, 1 - tm)

    pl.loop(0, held)(functools.partial(outer_rows, cross_slot))

    pieces = []
    for i in range(pairs):
        owner = window * pairs + i
        piece = pltpu.make_async_remote_copy(
            src_ref=outgoing.at[i],
            dst_ref=incoming.at[pair],
            send_sem=piece_send.at[i],
            recv_sem=piece_recv.at[pair],
            device_id=device(tm, owner),
            device_id_type=pl.DeviceIdType.MESH,
        )
        pieces.append((owner, piece))

    tall, cut = -(-chunk // 16) * 16, -(-chunk // 32) * 16
    for q in range(4):

        @pl.when(quarter == q)
        def _():
            for i in range(pairs):
                base = q * per_window - starts[q] * CH + i * chunk
                outgoing[i, 0:chunk, :] = filt[base : base + chunk, 0:128].astype(bf16)
                outgoing[i, tall : tall + cut, 0:64] = filt[base : base + cut, 128:CH].astype(bf16)
                outgoing[i, tall : tall + chunk - cut, 64:128] = filt[
                    base + cut : base + chunk, 128:CH
                ].astype(bf16)
                owner, piece = pieces[i]

                @pl.when(owner != row)
                def _():
                    piece.start()

                @pl.when(owner == row)
                def _():
                    incoming[pair] = outgoing[i]

    @pl.when(has_outer)
    def _():
        arrived(1, cot_slot, tm)
        edge.start()
        unpack(1, cot_slot, tm)

    @pl.when(has_outer)
    def _():
        arrived(1, cot_slot, 1 - tm)
        unpack(1, cot_slot, 1 - tm)

    convolve(2 * side, 2 - 2 * side, False)

    for frame in range(2):
        span = pl.ds(frame * WIDTH, WIDTH)
        inner = pl.ds(8, WIDTH)
        pad[inner, :] = fwd[0, span, :]
        value = fwd[1, span, :] + pad[7 : WIDTH + 7, :]
        pad[inner, :] = fwd[2, span, :]
        value = value + pad[9 : WIDTH + 9, :]
        out_ref[span, :] = value.astype(bf16)
        pad[inner, :] = bwd[0, span, :]
        value = bwd[1, span, :] + pad[9 : WIDTH + 9, :]
        pad[inner, :] = bwd[2, span, :]
        value = value + pad[7 : WIDTH + 7, :]
        x = x_ref[span, :].astype(f32)
        sigma = 1.0 / (1.0 + jnp.exp(-x))
        ig_ref[span, :] = (value * sigma * (1.0 + x * (1.0 - sigma))).astype(bf16)

    for source in range(pairs):
        from_row = 2 * source + (row // pairs + source) % 2

        @pl.when(from_row != row)
        def _():
            pltpu.make_async_remote_copy(
                src_ref=outgoing.at[0],
                dst_ref=incoming.at[source],
                send_sem=piece_send.at[0],
                recv_sem=piece_recv.at[source],
                device_id=sibling,
                device_id_type=pl.DeviceIdType.MESH,
            ).wait_recv()

    total = incoming[0].astype(f32)
    for source in range(1, pairs):
        total = total + incoming[source].astype(f32)
    total = (total / scale).astype(bf16)
    fg_ref[:, 0:128] = total[0:chunk]
    fg_ref[0:cut, 128:CH] = total[tall : tall + cut, 0:64]
    fg_ref[cut:chunk, 128:CH] = total[tall : tall + chunk - cut, 64:128]

    for copy in straight + onward:
        copy.wait_send()

    @pl.when(has_outer)
    def _():
        for copy in outward:
            copy.wait_send()
        edge.wait_send()
        cross.wait_send()

    @pl.when(has_same)
    def _():
        same.wait_send()

    for owner, piece in pieces:

        @pl.when(owner != row)
        def _():
            piece.wait_send()


def fused(inputs, weight, cotangent):
    frames, rows = inputs.shape[:2]
    tm_size, row_size = lax.axis_size("tm"), lax.axis_size("row")
    pairs = row_size // 2
    chunk = TAPS * CH // (2 * row_size)
    scale = frames * tm_size * rows * row_size
    quarter_rows = pairs * chunk
    held = max(
        -(-(q + 1) * quarter_rows // CH) - q * quarter_rows // CH for q in range(4)
    )
    piece_rows = -(-chunk // 16) * 16 + -(-chunk // 32) * 16
    vmem = pl.BlockSpec(memory_space=pltpu.VMEM)
    bf16, f32 = jnp.bfloat16, jnp.float32
    out, ig, fg = pl.pallas_call(
        functools.partial(fused_kernel, pairs, chunk, float(scale)),
        out_shape=(
            jax.ShapeDtypeStruct((BLOCK, CH), bf16),
            jax.ShapeDtypeStruct((BLOCK, CH), bf16),
            jax.ShapeDtypeStruct((chunk, CH), bf16),
        ),
        in_specs=[vmem, pl.BlockSpec(memory_space=pltpu.HBM), vmem],
        out_specs=(vmem, vmem, vmem),
        scratch_shapes=[
            pltpu.VMEM((4, 3 * BLOCK, CH), bf16),
            pltpu.VMEM((4, 3 * BLOCK, CH), bf16),
            pltpu.VMEM((2, 4, 2, PACKED, 128), bf16),
            pltpu.VMEM((CH, TAPS * CH), bf16),
            pltpu.VMEM((TAPS, CH, CH), bf16),
            pltpu.VMEM((3, 2, 2 * BLOCK, CH), bf16),
            pltpu.VMEM((held * CH, CH), f32),
            pltpu.VMEM((pairs, piece_rows, 128), bf16),
            pltpu.VMEM((pairs, piece_rows, 128), bf16),
            pltpu.VMEM((3, BLOCK, CH), f32),
            pltpu.VMEM((3, BLOCK, CH), f32),
            pltpu.VMEM((WIDTH + 16, CH), f32),
            pltpu.SemaphoreType.DMA,
            pltpu.SemaphoreType.DMA((12,)),
            pltpu.SemaphoreType.DMA((2, 4, 2)),
            pltpu.SemaphoreType.DMA((pairs,)),
            pltpu.SemaphoreType.DMA((pairs,)),
        ],
        compiler_params=pltpu.CompilerParams(
            collective_id=0, has_side_effects=True, vmem_limit_bytes=48 * 1024 * 1024
        ),
    )(inputs.reshape(BLOCK, CH), weight.T, cotangent.reshape(BLOCK, CH))
    shape = (frames, rows, WIDTH * CH)
    return out.reshape(shape), ig.reshape(shape), fg.reshape(-1)


def passed_along(array, axis, by):
    length = lax.axis_size(axis)
    pairs = [(i, i + by) for i in range(length) if 0 <= i + by < length]
    return lax.ppermute(array, axis, pairs)


def with_halo(array, sides, width):
    for axis, dim in sides:
        size, length = (lax.axis_size(axis), array.shape[dim])
        up = [(i, (i + 1) % size) for i in range(size - 1)]
        down = [(j, i) for i, j in up]
        last = lax.slice_in_dim(array, length - width, length, axis=dim)
        first = lax.slice_in_dim(array, 0, width, axis=dim)
        before = lax.ppermute(last, axis, up)
        after = lax.ppermute(first, axis, down)
        array = jnp.concatenate([before, array, after], axis=dim)
    return array


def on_device(inputs, weight, cotangent):
    frames = inputs.shape[0]
    rows = inputs.shape[1]
    act = jax.nn.silu(inputs.astype(jnp.float32)).astype(jnp.bfloat16)
    earlier = passed_along(act, "tm", 1)
    extended = jnp.concatenate([earlier, act], 0)
    extended = with_halo(extended, (("row", 1),), 1)
    extended = extended.reshape(frames + 2, rows + 2, WIDTH, CH)
    act_pad = jnp.pad(extended, ((0, 0), (0, 0), (1, 1), (0, 0)))
    cot_four = cotangent.reshape(frames, rows, WIDTH, CH)
    cot_flat = cot_four.reshape(-1, CH)
    output = jnp.zeros((frames * rows * WIDTH, CH), jnp.float32)
    blocks = []
    for step_t in range(3):
        for step_h in range(3):
            for step_w in range(3):
                offset = ((step_t * 3 + step_h) * 3 + step_w) * CH
                kernel = weight[offset : offset + CH]
                piece = act_pad[
                    step_t : step_t + frames, step_h : step_h + rows, step_w : step_w + WIDTH
                ].reshape(-1, CH)
                output = output + jnp.dot(piece, kernel, preferred_element_type=jnp.float32)
                blocks.append(
                    lax.dot_general(
                        piece,
                        cot_flat,
                        (((0,), (0,)), ((), ())),
                        preferred_element_type=jnp.float32,
                    )
                )
    spread = jnp.zeros((frames + 2, rows + 2, WIDTH + 2, CH), jnp.float32)
    for step_t in range(3):
        slab_weight = weight[step_t * 9 * CH : (step_t + 1) * 9 * CH]
        terms = lax.dot_general(
            cot_flat, slab_weight, (((1,), (1,)), ((), ())), preferred_element_type=jnp.float32
        )
        terms = terms.reshape(frames, rows, WIDTH, 9, CH)
        slab = jnp.zeros((frames, rows + 2, WIDTH + 2, CH), jnp.float32)
        for step_h in range(3):
            for step_w in range(3):
                slab = slab + jnp.pad(
                    terms[:, :, :, step_h * 3 + step_w],
                    ((0, 0), (step_h, 2 - step_h), (step_w, 2 - step_w), (0, 0)),
                )
        spread = spread + jnp.pad(slab, ((step_t, 2 - step_t), (0, 0), (0, 0), (0, 0)))
    inner = spread[:, :, 1 : WIDTH + 1]
    from_next = passed_along(inner[:, 0:1], "row", -1)
    from_prev = passed_along(inner[:, rows + 1 : rows + 2], "row", 1)
    center = inner[:, 1 : rows + 1]
    center = center.at[:, rows - 1 : rows].add(from_next)
    center = center.at[:, 0:1].add(from_prev)
    returned = passed_along(center[0:2], "tm", -1)
    grad_act = center[2:].at[frames - 2 :].add(returned).reshape(-1, CH)
    x_float = inputs.reshape(-1, CH).astype(jnp.float32)
    sigma = jax.nn.sigmoid(x_float)
    input_grad = (grad_act * sigma * (1.0 + x_float * (1.0 - sigma))).astype(jnp.bfloat16)
    local_filter = jnp.concatenate(blocks, 0).reshape(-1)
    frame_blocks = lax.axis_size("tm")
    row_blocks = lax.axis_size("row")
    scale = frames * frame_blocks * rows * row_blocks
    share = lax.psum_scatter(local_filter, ("tm", "row"), scatter_dimension=0, tiled=True)
    filter_grad = (share / scale).astype(jnp.bfloat16)
    shape = (frames, rows, WIDTH * CH)
    return (output.astype(jnp.bfloat16).reshape(shape), input_grad.reshape(shape), filter_grad)


def either(mesh, inputs, weight, cotangent):
    size = mesh.shape["row"]
    quads = mesh.shape["tm"] == 2 and size % 2 == 0 and TAPS * CH % (4 * size) == 0
    if quads and inputs.shape[:2] == (2, 1):
        return fused(inputs, weight, cotangent)
    return on_device(inputs, weight, cotangent)


def solution(mesh):
    placed = (P(("grp", "tm"), "row", None), P(), P(("grp", "tm"), "row", None))
    return jax.shard_map(
        functools.partial(either, mesh),
        mesh=mesh,
        in_specs=placed,
        out_specs=(
            P(("grp", "tm"), "row", None),
            P(("grp", "tm"), "row", None),
            P(("grp", "tm", "row")),
        ),
        check_vma=False,
    )
```
